256 devices in a mesh: seq: 32 (over y, x, core), fsdp: 8 (over z).
Axes of the slice: x: 4, y: 4, z: 8, core: 2. Of those that a mesh axis runs over, the one named last changes fastest.
Arguments:
- normed_block_input: bfloat16 [8, 4096, 8192], P('fsdp', 'seq'), may hold values from -6 to 6
- stored_rotated_queries: bfloat16 [8, 4096, 4096], P('fsdp', 'seq'), may hold values from -640 to 640
- stored_rotated_keys: bfloat16 [8, 4096, 512], P('fsdp', 'seq'), may hold values from -4 to 4
- attention_output_gradient: bfloat16 [8, 4096, 4096], P('fsdp', 'seq'), may hold values from -6 to 6
- frozen_value_weight: bfloat16 [8192, 512], P('fsdp'), may hold values from -0.0625 to 0.0625
- adapter_down_weight: bfloat16 [16, 8192], replicated, may hold values from -0.0625 to 0.0625
- adapter_up_weight: bfloat16 [16, 512], replicated, may hold values from -1.5 to 1.5
- packed_document_lengths: int32 [8, 8], P('fsdp'), may hold values from 1 to 1024, 4096 in all within a row
Outputs:
- input_gradient: bfloat16 [8, 4096, 8192], P('fsdp', 'seq')
- rotated_query_gradient: bfloat16 [8, 4096, 4096], P('fsdp', 'seq')
- rotated_key_gradient: bfloat16 [8, 4096, 512], P('fsdp', 'seq')
- adapter_down_gradient: float32 [16, 8192], replicated
- adapter_up_gradient: float32 [16, 512], replicated
The draws below stay inside these ranges and needn't reach their ends.
Inputs may be any that keep to these rules, and one draw needn't show every extreme that they name: `packed_document_lengths`: row g holds, in order, the lengths of the 8 documents packed into sequence g; they sum to 4096, and in every row the longest has exactly 1024 tokens.
All inputs are finite; a program needn't handle non-finite values.
Results may differ from the reference program's by a relative error of at most 0.0065.
Values may be sent and summed in bfloat16 or wider, within the bound.
A program may use at most 128 MiB of HBM per device.

```python
import math
import jax
import jax.numpy as jnp
import numpy as np
from jax import lax

MODEL_DIMENSION = 8192
HEAD_FEATURES = 128
QUERY_HEADS = 32
KEY_VALUE_HEADS = 4
ADAPTER_RANK = 16
DOCS = 8
SEQUENCE_TOKENS = 4096
TOKEN_COUNT = 32768
DOC_MOST = 1024
CQ = 4096
KEY_VALUE_WIDTH = 512
N_FSDP = 8


def paired_draw(key):
    base_key = jax.random.fold_in(key, 9173)
    key_query, random_key_split = jax.random.split(base_key, 2)
    queries = jnp.clip(jax.random.normal(key_query, (N_FSDP, SEQUENCE_TOKENS, QUERY_HEADS, HEAD_FEATURES), jnp.float32), -4.0, 4.0)
    complete_keys = jnp.clip(jax.random.normal(random_key_split, (N_FSDP, SEQUENCE_TOKENS, KEY_VALUE_HEADS, HEAD_FEATURES), jnp.float32), -4.0, 4.0)
    return (queries, complete_keys)


def draw_stored_rotated_queries(key, part):
    queries, complete_keys = paired_draw(key)
    return queries.reshape(N_FSDP, SEQUENCE_TOKENS, QUERY_HEADS * HEAD_FEATURES).astype(jnp.bfloat16)


def draw_stored_rotated_keys(key, part):
    queries, complete_keys = paired_draw(key)
    return complete_keys.reshape(N_FSDP, SEQUENCE_TOKENS, KEY_VALUE_HEADS * HEAD_FEATURES).astype(jnp.bfloat16)


def steps_of(key, dims, pieces, smallest, top_value):
    factor_of = 1.0
    for dim, parts in pieces:
        steps = jax.random.uniform(jax.random.fold_in(jax.random.fold_in(key, 6), dim), (parts,), jnp.float32, smallest / len(pieces), top_value / len(pieces))
        factor_of = factor_of * jnp.repeat(jnp.exp(steps), dims[dim] // parts).reshape((-1,) + (1,) * (len(dims) - 1 - dim))
    return factor_of


def split_up(amount, total, bound, slope):
    weights = [(1 << 20) // math.isqrt(standing ** slope) + 1 for standing in range(2, amount + 1)]
    spare, holding = total - bound - (amount - 1), [1] * (amount - 1)
    while spare > 0:
        free = [i for i in range(amount - 1) if holding[i] < bound]
        mass, remaining = sum([weights[i] for i in free]), spare
        for i in free:
            addition = min(bound - holding[i], max(1, remaining * weights[i] // mass), spare)
            holding[i] = holding[i] + addition
            spare = spare - addition
    return np.array([bound] + holding)


def uneven(stream_key, count, total, bound, skew):
    if count == 2:
        one = jax.random.randint(stream_key, (), max(1, total - bound), min(bound, total - 1) + 1)
        return jnp.stack([one, total - one])
    sizes = jnp.asarray(split_up(count, total, bound, skew), jnp.int32)
    twos = (count - 1) // 2
    giver, sink = sizes[1:1 + 2 * twos:2], sizes[2:2 + 2 * twos:2]
    slack = jnp.minimum(giver - 1, bound - sink)
    shifted = jax.random.randint(jax.random.fold_in(stream_key, 1), (twos,), 0, 1 << 20) % (slack + 1)
    sizes = sizes.at[1:1 + 2 * twos:2].set(giver - shifted).at[2:2 + 2 * twos:2].set(sink + shifted)
    return sizes[jax.random.permutation(jax.random.fold_in(stream_key, 2), count)]


def centred(key, dims, deviation, bound, cuts=(), kind=jnp.bfloat16):
    values = deviation * jax.random.normal(key, dims, jnp.float32)
    if cuts:
        values = values * steps_of(key, dims, cuts, -0.22, 0.18)
    return jnp.clip(values, -bound, bound).astype(kind)


def setup_inputs(seed: int = 0) -> dict:
    arg_keys = jax.random.split(jax.random.key(seed), 9)
    return {
        "normed_block_input": centred(arg_keys[0], (N_FSDP, SEQUENCE_TOKENS, MODEL_DIMENSION), 1.0, 6.0, ((0, 8), (1, 32))),
        "stored_rotated_queries": draw_stored_rotated_queries(jax.random.fold_in(arg_keys[8], 71), 0),
        "stored_rotated_keys": draw_stored_rotated_keys(jax.random.fold_in(arg_keys[8], 71), 0),
        "attention_output_gradient": centred(arg_keys[3], (N_FSDP, SEQUENCE_TOKENS, CQ), 1.0, 6.0, ((0, 8), (1, 32))),
        "frozen_value_weight": centred(arg_keys[4], (MODEL_DIMENSION, KEY_VALUE_WIDTH), MODEL_DIMENSION ** -0.5, 0.0625, ((0, 8),)),
        "adapter_down_weight": centred(arg_keys[5], (ADAPTER_RANK, MODEL_DIMENSION), MODEL_DIMENSION ** -0.5, 0.0625),
        "adapter_up_weight": centred(arg_keys[6], (ADAPTER_RANK, KEY_VALUE_WIDTH), ADAPTER_RANK ** -0.5, 1.5),
        "packed_document_lengths": jax.vmap(lambda own: uneven(own, DOCS, SEQUENCE_TOKENS, DOC_MOST, 2))(jax.random.split(arg_keys[7], N_FSDP)).reshape((N_FSDP, DOCS)).astype(jnp.int32),
    }


ADAPTER_SCALE = 2.0
NEG_FILL = -1e30


def segment_ids(lengths_row, length):
    bounds = jnp.cumsum(lengths_row)
    places = jnp.arange(length, dtype=jnp.int32)
    return jnp.sum((places[:, None] >= bounds[None, :]).astype(jnp.int32), axis=1)


def head_backward(query_head, key_head, value_head, grad_head, allowed):
    inverse = HEAD_FEATURES ** -0.5
    scores = jnp.dot(query_head, key_head.T, preferred_element_type=jnp.float32) * inverse
    scores = jnp.where(allowed, scores, NEG_FILL)
    row_peak = jnp.max(scores, axis=1, keepdims=True)
    weights = jnp.exp(scores - row_peak)
    probs_full = weights / jnp.sum(weights, axis=1, keepdims=True)
    probs_low = probs_full.astype(jnp.bfloat16)
    grad_probs = jnp.dot(grad_head, value_head.T, preferred_element_type=jnp.float32)
    row_delta = jnp.sum(probs_full * grad_probs, axis=1, keepdims=True)
    grad_scores = (probs_full * (grad_probs - row_delta)).astype(jnp.bfloat16)
    grad_query = jnp.dot(grad_scores, key_head, preferred_element_type=jnp.float32) * inverse
    key_gradient_rows = jnp.dot(grad_scores.T, query_head, preferred_element_type=jnp.float32) * inverse
    value_gradient_rows = jnp.dot(probs_low.T, grad_head, preferred_element_type=jnp.float32)
    return grad_query, key_gradient_rows, value_gradient_rows


def group_backward(group_item):
    query_rows, key_token_rows, value_token_rows, grad_rows, lengths_row = group_item
    queries_per_group = QUERY_HEADS // KEY_VALUE_HEADS
    segments = segment_ids(lengths_row, SEQUENCE_TOKENS)
    places = jnp.arange(SEQUENCE_TOKENS, dtype=jnp.int32)
    allowed = (places[None, :] <= places[:, None]) & (segments[:, None] == segments[None, :])
    query_heads = query_rows.reshape(SEQUENCE_TOKENS, QUERY_HEADS, HEAD_FEATURES).transpose(1, 0, 2)
    grad_heads = grad_rows.reshape(SEQUENCE_TOKENS, QUERY_HEADS, HEAD_FEATURES).transpose(1, 0, 2)
    key_head_split = jnp.repeat(key_token_rows.reshape(SEQUENCE_TOKENS, KEY_VALUE_HEADS, HEAD_FEATURES).transpose(1, 0, 2), queries_per_group, axis=0)
    value_head_split = jnp.repeat(value_token_rows.reshape(SEQUENCE_TOKENS, KEY_VALUE_HEADS, HEAD_FEATURES).transpose(1, 0, 2), queries_per_group, axis=0)

    def one_head(head_item):
        return head_backward(head_item[0], head_item[1], head_item[2], head_item[3], allowed)

    grad_query, key_gradient_rows, value_gradient_rows = lax.map(one_head, (query_heads, key_head_split, value_head_split, grad_heads))
    grad_query = grad_query.transpose(1, 0, 2).reshape(SEQUENCE_TOKENS, QUERY_HEADS * HEAD_FEATURES)
    key_gradient_rows = key_gradient_rows.reshape(KEY_VALUE_HEADS, queries_per_group, SEQUENCE_TOKENS, HEAD_FEATURES).sum(axis=1).transpose(1, 0, 2).reshape(SEQUENCE_TOKENS, KEY_VALUE_HEADS * HEAD_FEATURES)
    value_gradient_rows = value_gradient_rows.reshape(KEY_VALUE_HEADS, queries_per_group, SEQUENCE_TOKENS, HEAD_FEATURES).sum(axis=1).transpose(1, 0, 2).reshape(SEQUENCE_TOKENS, KEY_VALUE_HEADS * HEAD_FEATURES)
    return grad_query, key_gradient_rows, value_gradient_rows


def reference(normed_block_input, stored_rotated_queries, stored_rotated_keys, attention_output_gradient, frozen_value_weight, adapter_down_weight, adapter_up_weight, packed_document_lengths):
    hidden_activations = normed_block_input.reshape(TOKEN_COUNT, MODEL_DIMENSION)
    adapter_projection = lax.dot_general(hidden_activations, adapter_down_weight, (((1,), (1,)), ((), ())), preferred_element_type=jnp.float32)
    up_widened = adapter_up_weight.astype(jnp.float32)
    adapter_values = (jnp.dot(hidden_activations, frozen_value_weight, preferred_element_type=jnp.float32)
                  + ADAPTER_SCALE * jnp.dot(adapter_projection, up_widened, precision=lax.Precision.HIGHEST)).astype(jnp.bfloat16)
    adapter_values = adapter_values.reshape(N_FSDP, SEQUENCE_TOKENS, KEY_VALUE_HEADS * HEAD_FEATURES)
    grad_query, key_gradient_rows, value_gradient_rows = lax.map(group_backward, (stored_rotated_queries, stored_rotated_keys, adapter_values, attention_output_gradient, packed_document_lengths))
    value_gradient_matrix = value_gradient_rows.reshape(TOKEN_COUNT, KEY_VALUE_HEADS * HEAD_FEATURES)
    value_grad_low = value_gradient_matrix.astype(jnp.bfloat16)
    adapter_rank_gradient = ADAPTER_SCALE * lax.dot_general(value_gradient_matrix, up_widened, (((1,), (1,)), ((), ())), precision=lax.Precision.HIGHEST)
    reduced_rank_gradient = adapter_rank_gradient.astype(jnp.bfloat16)
    input_gradient = (lax.dot_general(value_grad_low, frozen_value_weight, (((1,), (1,)), ((), ())), preferred_element_type=jnp.float32)
                + jnp.dot(reduced_rank_gradient, adapter_down_weight, preferred_element_type=jnp.float32)).astype(jnp.bfloat16)
    adapter_down_gradient = lax.dot_general(reduced_rank_gradient, hidden_activations, (((0,), (0,)), ((), ())), preferred_element_type=jnp.float32) / TOKEN_COUNT
    adapter_up_gradient = ADAPTER_SCALE * jnp.dot(adapter_projection.T, value_gradient_matrix, precision=lax.Precision.HIGHEST) / TOKEN_COUNT
    return (input_gradient.reshape(N_FSDP, SEQUENCE_TOKENS, MODEL_DIMENSION), grad_query.astype(jnp.bfloat16), key_gradient_rows.astype(jnp.bfloat16),
            adapter_down_gradient, adapter_up_gradient)
```

```python
import functools

import jax
import jax.numpy as jnp
from jax import lax
from jax.experimental import pallas as pl
from jax.experimental.pallas import tpu as pltpu
from jax.sharding import PartitionSpec as P

HEAD_FEATURES = 128
QUERY_HEADS = 32
KEY_VALUE_HEADS = 4


ADAPTER_SCALE = 2.0
NEG_FILL = -1e30


MESH = pl.DeviceIdType.MESH
SUM_ROWS = 24
SUM_LANES = 256


def sum_kernel(
    chips,
    depth,
    parts_ref,
    out_ref,
    pair_in,
    pair_total,
    chip_in,
    chip_total,
    depth_in,
    pair_send,
    pair_recv,
    chip_send,
    chip_recv,
    depth_send,
    depth_recv,
    give_send,
    give_recv,
    hand_send,
    hand_recv,
):
    me = lax.axis_index("seq")
    layer = lax.axis_index("fsdp")
    chip = me // 2
    core = lax.rem(me, 2)
    partner = chip * 2 + 1 - core

    def chip_peer(offset):
        return lax.rem(chip + offset, chips) * 2 + core

    def depth_peer(offset):
        return lax.rem(layer + offset, depth)

    barrier = pltpu.get_barrier_semaphore()
    pl.semaphore_signal(barrier, inc=1, device_id={"seq": partner}, device_id_type=MESH)
    for offset in range(1, chips):
        pl.semaphore_signal(
            barrier, inc=1, device_id={"seq": chip_peer(offset)}, device_id_type=MESH
        )
    for offset in range(1, depth):
        pl.semaphore_signal(
            barrier, inc=1, device_id={"fsdp": depth_peer(offset)}, device_id_type=MESH
        )
    pl.semaphore_wait(barrier, chips + depth - 1)

    pair = pltpu.make_async_remote_copy(
        src_ref=parts_ref.at[:, 1 - core],
        dst_ref=pair_in,
        send_sem=pair_send,
        recv_sem=pair_recv,
        device_id={"seq": partner},
        device_id_type=MESH,
    )
    pair.start()
    pair.wait()

    def add_pair(index, carry):
        pair_total[index] = parts_ref[index, core] + pair_in[index]
        return carry

    lax.fori_loop(0, chips, add_pair, 0)

    copies = []
    for offset in range(1, chips):
        target = lax.rem(chip + offset, chips)
        copy = pltpu.make_async_remote_copy(
            src_ref=pair_total.at[target],
            dst_ref=chip_in.at[offset - 1],
            send_sem=chip_send.at[offset - 1],
            recv_sem=chip_recv.at[offset - 1],
            device_id={"seq": chip_peer(offset)},
            device_id_type=MESH,
        )
        copy.start()
        copies.append(copy)
    for copy in copies:
        copy.wait()
    total = pair_total[chip]
    for offset in range(chips - 1):
        total = total + chip_in[offset]
    chip_total[0] = total

    copies = []
    for offset in range(1, depth):
        copy = pltpu.make_async_remote_copy(
            src_ref=chip_total.at[0],
            dst_ref=depth_in.at[offset - 1],
            send_sem=depth_send.at[offset - 1],
            recv_sem=depth_recv.at[offset - 1],
            device_id={"fsdp": depth_peer(offset)},
            device_id_type=MESH,
        )
        copy.start()
        copies.append(copy)
    for copy in copies:
        copy.wait()
    rows = [total]
    for offset in range(depth - 1):
        rows.append(depth_in[offset])
    final = rows[0]
    for row in rows[1:]:
        final = final + row
    out_ref[chip, core] = final

    gives = []
    for offset in range(1, chips):
        copy = pltpu.make_async_remote_copy(
            src_ref=out_ref.at[chip, core],
            dst_ref=out_ref.at[chip, core],
            send_sem=give_send.at[offset - 1],
            recv_sem=give_recv.at[offset - 1],
            device_id={"seq": chip_peer(offset)},
            device_id_type=MESH,
        )
        copy.start()
        gives.append(copy)
    hands = []
    for offset in range(chips):
        owner = lax.rem(chip + chips - offset, chips)
        if offset:
            got = pltpu.make_async_remote_copy(
                src_ref=out_ref.at[owner, core],
                dst_ref=out_ref.at[owner, core],
                send_sem=give_send.at[offset - 1],
                recv_sem=give_recv.at[offset - 1],
                device_id={"seq": chip_peer(offset)},
                device_id_type=MESH,
            )
            got.wait_recv()
        hand = pltpu.make_async_remote_copy(
            src_ref=out_ref.at[owner, core],
            dst_ref=out_ref.at[owner, core],
            send_sem=hand_send.at[offset],
            recv_sem=hand_recv.at[offset],
            device_id={"seq": partner},
            device_id_type=MESH,
        )
        hand.start()
        hands.append(hand)
    for copy in gives:
        copy.wait_send()
    for offset, hand in enumerate(hands):
        owner = lax.rem(chip + chips - offset, chips)
        hand.wait_send()
        pltpu.make_async_remote_copy(
            src_ref=out_ref.at[owner, 1 - core],
            dst_ref=out_ref.at[owner, 1 - core],
            send_sem=hand_send.at[offset],
            recv_sem=hand_recv.at[offset],
            device_id={"seq": partner},
            device_id_type=MESH,
        ).wait_recv()


def sum_over_mesh(down_shard, up_shard, seq_count, fsdp_count):
    chips = seq_count // 2
    rank, width = down_shard.shape
    blocks = down_shard.reshape(rank, seq_count, SUM_LANES).transpose(1, 0, 2)
    ups = up_shard.reshape(seq_count, 1, SUM_LANES)
    parts = jnp.concatenate(
        [blocks, ups, jnp.zeros((seq_count, SUM_ROWS - rank - 1, SUM_LANES), jnp.float32)], axis=1
    ).reshape(chips, 2, SUM_ROWS, SUM_LANES)
    block = (SUM_ROWS, SUM_LANES)
    sems = pltpu.SemaphoreType.DMA
    summed = pl.pallas_call(
        functools.partial(sum_kernel, chips, fsdp_count),
        out_shape=jax.ShapeDtypeStruct(parts.shape, jnp.float32),
        in_specs=[pl.BlockSpec(memory_space=pltpu.VMEM)],
        out_specs=pl.BlockSpec(memory_space=pltpu.VMEM),
        scratch_shapes=[
            pltpu.VMEM((chips,) + block, jnp.float32),
            pltpu.VMEM((chips,) + block, jnp.float32),
            pltpu.VMEM((chips - 1,) + block, jnp.float32),
            pltpu.VMEM((1,) + block, jnp.float32),
            pltpu.VMEM((fsdp_count - 1,) + block, jnp.float32),
            sems,
            sems,
            sems((chips - 1,)),
            sems((chips - 1,)),
            sems((fsdp_count - 1,)),
            sems((fsdp_count - 1,)),
            sems((chips - 1,)),
            sems((chips - 1,)),
            sems((chips,)),
            sems((chips,)),
        ],
        compiler_params=pltpu.CompilerParams(collective_id=0, has_side_effects=True),
        name="adapter_sum",
    )(parts).reshape(seq_count, SUM_ROWS, SUM_LANES)
    down = summed[:, :rank].transpose(1, 0, 2).reshape(rank, width)
    up = summed[:, rank].reshape(up_shard.shape)
    return down, up


def contract_trailing(left_rows, right_rows):
    return lax.dot_general(
        left_rows, right_rows, (((1,), (1,)), ((), ())), preferred_element_type=jnp.float32
    )


def body(
    normed_block_input,
    stored_rotated_queries,
    stored_rotated_keys,
    attention_output_gradient,
    frozen_value_weight,
    adapter_down_weight,
    adapter_up_weight,
    packed_document_lengths,
):
    token_rows = normed_block_input.shape[1]
    model_features = normed_block_input.shape[2]
    hidden_activations = normed_block_input.reshape(token_rows, model_features)
    seq_count = lax.axis_size("seq")
    fsdp_count = lax.axis_size("fsdp")
    queries_per_group = QUERY_HEADS // KEY_VALUE_HEADS
    key_value_features = KEY_VALUE_HEADS * HEAD_FEATURES
    inverse = HEAD_FEATURES ** (-0.5)
    adapter_projection = contract_trailing(hidden_activations, adapter_down_weight)
    up_widened = adapter_up_weight.astype(jnp.float32)
    adapter_maps = ADAPTER_SCALE * jnp.dot(
        adapter_projection, up_widened, precision=lax.Precision.HIGHEST
    )
    base_value = jnp.dot(
        hidden_activations,
        lax.all_gather(frozen_value_weight, "fsdp", axis=0, tiled=True),
        preferred_element_type=jnp.float32,
    )
    adapter_values = (base_value + adapter_maps).astype(jnp.bfloat16)
    shaped = (token_rows, QUERY_HEADS, HEAD_FEATURES)
    key_broadcast = jnp.repeat(
        stored_rotated_keys.reshape(token_rows, KEY_VALUE_HEADS, HEAD_FEATURES),
        queries_per_group,
        axis=1,
    )
    value_broadcast = jnp.repeat(
        adapter_values.reshape(token_rows, KEY_VALUE_HEADS, HEAD_FEATURES),
        queries_per_group,
        axis=1,
    )
    head_query, head_key, head_value, head_grad = (
        lax.all_to_all(
            stored_rotated_queries.reshape(shaped), "seq", split_axis=1, concat_axis=0, tiled=True
        ),
        lax.all_to_all(key_broadcast, "seq", split_axis=1, concat_axis=0, tiled=True),
        lax.all_to_all(value_broadcast, "seq", split_axis=1, concat_axis=0, tiled=True),
        lax.all_to_all(
            attention_output_gradient.reshape(shaped),
            "seq",
            split_axis=1,
            concat_axis=0,
            tiled=True,
        ),
    )
    seq_len = head_query.shape[0]
    local_heads = head_query.shape[1]
    block_rows = min(512, seq_len)
    key_reach = block_rows + seq_len // 4
    bounds = jnp.cumsum(packed_document_lengths[0])
    places = jnp.arange(seq_len, dtype=jnp.int32)
    segments = jnp.sum((places[:, None] >= bounds[None, :]).astype(jnp.int32), axis=1)
    grad_keys = jnp.zeros((seq_len, local_heads, HEAD_FEATURES), jnp.float32)
    grad_values = jnp.zeros((seq_len, local_heads, HEAD_FEATURES), jnp.float32)
    query_parts = []
    for block_index in range(seq_len // block_rows):
        first_row = block_index * block_rows
        finish = first_row + block_rows
        opening = max(0, finish - key_reach)
        query_block = head_query[first_row:finish]
        grad_block = head_grad[first_row:finish]
        key_block = head_key[opening:finish]
        value_block = head_value[opening:finish]
        scores = (
            jnp.einsum("qhd,khd->hqk", query_block, key_block, preferred_element_type=jnp.float32)
            * inverse
        )
        allowed = (places[opening:finish][None, :] <= places[first_row:finish][:, None]) & (
            segments[opening:finish][None, :] == segments[first_row:finish][:, None]
        )
        scores = jnp.where(allowed[None], scores, NEG_FILL)
        row_peak = jnp.max(scores, axis=2, keepdims=True)
        weights = jnp.exp(scores - row_peak)
        probs_full = weights / jnp.sum(weights, axis=2, keepdims=True)
        probs_low = probs_full.astype(jnp.bfloat16)
        grad_probs = jnp.einsum(
            "qhd,khd->hqk", grad_block, value_block, preferred_element_type=jnp.float32
        )
        row_delta = jnp.sum(probs_full * grad_probs, axis=2, keepdims=True)
        grad_scores = (probs_full * (grad_probs - row_delta)).astype(jnp.bfloat16)
        query_parts.append(
            jnp.einsum("hqk,khd->qhd", grad_scores, key_block, preferred_element_type=jnp.float32)
            * inverse
        )
        key_part = (
            jnp.einsum("hqk,qhd->khd", grad_scores, query_block, preferred_element_type=jnp.float32)
            * inverse
        )
        value_part = jnp.einsum(
            "hqk,qhd->khd", probs_low, grad_block, preferred_element_type=jnp.float32
        )
        grad_keys = lax.dynamic_update_slice_in_dim(
            grad_keys, grad_keys[opening:finish] + key_part, opening, 0
        )
        grad_values = lax.dynamic_update_slice_in_dim(
            grad_values, grad_values[opening:finish] + value_part, opening, 0
        )
    grad_queries = jnp.concatenate(query_parts, axis=0).astype(jnp.bfloat16)
    token_query = lax.all_to_all(grad_queries, "seq", split_axis=0, concat_axis=1, tiled=True)
    rotated_query_gradient = token_query.reshape(1, token_rows, QUERY_HEADS * HEAD_FEATURES)
    token_key_matrix, token_value_matrix = (
        lax.all_to_all(grad_keys, "seq", split_axis=0, concat_axis=1, tiled=True),
        lax.all_to_all(grad_values, "seq", split_axis=0, concat_axis=1, tiled=True),
    )
    per_key_value_head = token_key_matrix.shape[1] // KEY_VALUE_HEADS
    rotated_key_gradient = (
        token_key_matrix.reshape(token_rows, KEY_VALUE_HEADS, per_key_value_head, HEAD_FEATURES)
        .sum(axis=2)
        .reshape(1, token_rows, key_value_features)
        .astype(jnp.bfloat16)
    )
    value_gradient_matrix = (
        token_value_matrix.reshape(token_rows, KEY_VALUE_HEADS, per_key_value_head, HEAD_FEATURES)
        .sum(axis=2)
        .reshape(token_rows, key_value_features)
    )
    value_grad_low = value_gradient_matrix.astype(jnp.bfloat16)
    adapter_rank_gradient = ADAPTER_SCALE * lax.dot_general(
        value_gradient_matrix, up_widened, (((1,), (1,)), ((), ())), precision=lax.Precision.HIGHEST
    )
    reduced_rank_gradient = adapter_rank_gradient.astype(jnp.bfloat16)
    frozen_path_gradient = contract_trailing(
        value_grad_low, lax.all_gather(frozen_value_weight, "fsdp", axis=0, tiled=True)
    )
    input_gradient = (
        frozen_path_gradient
        + jnp.dot(reduced_rank_gradient, adapter_down_weight, preferred_element_type=jnp.float32)
    ).astype(jnp.bfloat16)
    overall_token_count = token_rows * seq_count * fsdp_count
    down_shard = (
        lax.dot_general(
            reduced_rank_gradient,
            hidden_activations,
            (((0,), (0,)), ((), ())),
            preferred_element_type=jnp.float32,
        )
        / overall_token_count
    )
    up_shard = (
        ADAPTER_SCALE
        * jnp.dot(adapter_projection.T, value_gradient_matrix, precision=lax.Precision.HIGHEST)
        / overall_token_count
    )
    adapter_down_gradient, adapter_up_gradient = sum_over_mesh(
        down_shard, up_shard, seq_count, fsdp_count
    )
    return (
        input_gradient.reshape(1, token_rows, model_features),
        rotated_query_gradient,
        rotated_key_gradient,
        adapter_down_gradient,
        adapter_up_gradient,
    )


def solution(mesh):
    placed = (
        P("fsdp", "seq", None),
        P("fsdp", "seq", None),
        P("fsdp", "seq", None),
        P("fsdp", "seq", None),
        P("fsdp", None),
        P(),
        P(),
        P("fsdp", None),
    )
    return jax.shard_map(
        body,
        mesh=mesh,
        in_specs=placed,
        out_specs=(
            P("fsdp", "seq", None),
            P("fsdp", "seq", None),
            P("fsdp", "seq", None),
            P(),
            P(),
        ),
        check_vma=False,
    )
```

```python
import functools

import jax
import jax.numpy as jnp
from jax import lax
from jax.experimental import pallas as pl
from jax.experimental.pallas import tpu as pltpu
from jax.sharding import PartitionSpec as P

HEAD_FEATURES = 128


ADAPTER_SCALE = 2.0
NEG_FILL = -1e30
LOG2_E = 1.4426950408889634
DOCS = 8
DOC_MOST = 1024


MESH = pl.DeviceIdType.MESH
SUM_ROWS = 24
SUM_LANES = 256


def sum_kernel(
    chips,
    depth,
    parts_ref,
    out_ref,
    pair_in,
    pair_total,
    chip_in,
    chip_total,
    depth_in,
    pair_send,
    pair_recv,
    chip_send,
    chip_recv,
    depth_send,
    depth_recv,
    give_send,
    give_recv,
    hand_send,
    hand_recv,
):
    me = lax.axis_index("seq")
    layer = lax.axis_index("fsdp")
    chip = me // 2
    core = lax.rem(me, 2)
    partner = chip * 2 + 1 - core

    def chip_peer(offset):
        return lax.rem(chip + offset, chips) * 2 + core

    def depth_peer(offset):
        return lax.rem(layer + offset, depth)

    barrier = pltpu.get_barrier_semaphore()
    pl.semaphore_signal(barrier, inc=1, device_id={"seq": partner}, device_id_type=MESH)
    for offset in range(1, chips):
        pl.semaphore_signal(
            barrier, inc=1, device_id={"seq": chip_peer(offset)}, device_id_type=MESH
        )
    for offset in range(1, depth):
        pl.semaphore_signal(
            barrier, inc=1, device_id={"fsdp": depth_peer(offset)}, device_id_type=MESH
        )
    pl.semaphore_wait(barrier, chips + depth - 1)

    pair = pltpu.make_async_remote_copy(
        src_ref=parts_ref.at[:, 1 - core],
        dst_ref=pair_in,
        send_sem=pair_send,
        recv_sem=pair_recv,
        device_id={"seq": partner},
        device_id_type=MESH,
    )
    pair.start()
    pair.wait()

    def add_pair(index, carry):
        pair_total[index] = parts_ref[index, core] + pair_in[index]
        return carry

    lax.fori_loop(0, chips, add_pair, 0)

    copies = []
    for offset in range(1, chips):
        target = lax.rem(chip + offset, chips)
        copy = pltpu.make_async_remote_copy(
            src_ref=pair_total.at[target],
            dst_ref=chip_in.at[offset - 1],
            send_sem=chip_send.at[offset - 1],
            recv_sem=chip_recv.at[offset - 1],
            device_id={"seq": chip_peer(offset)},
            device_id_type=MESH,
        )
        copy.start()
        copies.append(copy)
    for copy in copies:
        copy.wait()
    total = pair_total[chip]
    for offset in range(chips - 1):
        total = total + chip_in[offset]
    chip_total[0] = total

    copies = []
    for offset in range(1, depth):
        copy = pltpu.make_async_remote_copy(
            src_ref=chip_total.at[0],
            dst_ref=depth_in.at[offset - 1],
            send_sem=depth_send.at[offset - 1],
            recv_sem=depth_recv.at[offset - 1],
            device_id={"fsdp": depth_peer(offset)},
            device_id_type=MESH,
        )
        copy.start()
        copies.append(copy)
    for copy in copies:
        copy.wait()
    rows = [total]
    for offset in range(depth - 1):
        rows.append(depth_in[offset])
    final = rows[0]
    for row in rows[1:]:
        final = final + row
    out_ref[chip, core] = final

    gives = []
    for offset in range(1, chips):
        copy = pltpu.make_async_remote_copy(
            src_ref=out_ref.at[chip, core],
            dst_ref=out_ref.at[chip, core],
            send_sem=give_send.at[offset - 1],
            recv_sem=give_recv.at[offset - 1],
            device_id={"seq": chip_peer(offset)},
            device_id_type=MESH,
        )
        copy.start()
        gives.append(copy)
    hands = []
    for offset in range(chips):
        owner = lax.rem(chip + chips - offset, chips)
        if offset:
            got = pltpu.make_async_remote_copy(
                src_ref=out_ref.at[owner, core],
                dst_ref=out_ref.at[owner, core],
                send_sem=give_send.at[offset - 1],
                recv_sem=give_recv.at[offset - 1],
                device_id={"seq": chip_peer(offset)},
                device_id_type=MESH,
            )
            got.wait_recv()
        hand = pltpu.make_async_remote_copy(
            src_ref=out_ref.at[owner, core],
            dst_ref=out_ref.at[owner, core],
            send_sem=hand_send.at[offset],
            recv_sem=hand_recv.at[offset],
            device_id={"seq": partner},
            device_id_type=MESH,
        )
        hand.start()
        hands.append(hand)
    for copy in gives:
        copy.wait_send()
    for offset, hand in enumerate(hands):
        owner = lax.rem(chip + chips - offset, chips)
        hand.wait_send()
        pltpu.make_async_remote_copy(
            src_ref=out_ref.at[owner, 1 - core],
            dst_ref=out_ref.at[owner, 1 - core],
            send_sem=hand_send.at[offset],
            recv_sem=hand_recv.at[offset],
            device_id={"seq": partner},
            device_id_type=MESH,
        ).wait_recv()


def sum_over_mesh(down_shard, up_shard, seq_count, fsdp_count):
    chips = seq_count // 2
    rank, width = down_shard.shape
    blocks = down_shard.reshape(rank, seq_count, SUM_LANES).transpose(1, 0, 2)
    ups = up_shard.reshape(seq_count, 1, SUM_LANES)
    parts = jnp.concatenate(
        [blocks, ups, jnp.zeros((seq_count, SUM_ROWS - rank - 1, SUM_LANES), jnp.float32)], axis=1
    ).reshape(chips, 2, SUM_ROWS, SUM_LANES)
    block = (SUM_ROWS, SUM_LANES)
    sems = pltpu.SemaphoreType.DMA
    summed = pl.pallas_call(
        functools.partial(sum_kernel, chips, fsdp_count),
        out_shape=jax.ShapeDtypeStruct(parts.shape, jnp.float32),
        in_specs=[pl.BlockSpec(memory_space=pltpu.VMEM)],
        out_specs=pl.BlockSpec(memory_space=pltpu.VMEM),
        scratch_shapes=[
            pltpu.VMEM((chips,) + block, jnp.float32),
            pltpu.VMEM((chips,) + block, jnp.float32),
            pltpu.VMEM((chips - 1,) + block, jnp.float32),
            pltpu.VMEM((1,) + block, jnp.float32),
            pltpu.VMEM((fsdp_count - 1,) + block, jnp.float32),
            sems,
            sems,
            sems((chips - 1,)),
            sems((chips - 1,)),
            sems((fsdp_count - 1,)),
            sems((fsdp_count - 1,)),
            sems((chips - 1,)),
            sems((chips - 1,)),
            sems((chips,)),
            sems((chips,)),
        ],
        compiler_params=pltpu.CompilerParams(collective_id=0, has_side_effects=True),
        name="adapter_sum",
    )(parts).reshape(seq_count, SUM_ROWS, SUM_LANES)
    down = summed[:, :rank].transpose(1, 0, 2).reshape(rank, width)
    up = summed[:, rank].reshape(up_shard.shape)
    return down, up


def halo_copies(source_ref, target_ref, send_sems, recv_sems, chips, reach):
    me = lax.axis_index("seq")
    chip = me // 2
    core = lax.rem(me, 2)
    rows, width = source_ref.shape
    half = width // 2
    own = None
    remote = []
    for behind in range(reach + 1):
        for cross in range(2):
            to_core = core if cross == 0 else 1 - core
            lanes = pl.ds(pl.multiple_of(to_core * half, half), half)
            slot = pl.multiple_of(((reach - behind) * 2 + core) * rows, rows)
            source = source_ref.at[:, lanes]
            target = target_ref.at[pl.ds(slot, rows), :]
            index = behind * 2 + cross
            if index == 0:
                own = pltpu.make_async_copy(source, target, send_sems.at[0])
            else:
                remote.append(
                    pltpu.make_async_remote_copy(
                        src_ref=source,
                        dst_ref=target,
                        send_sem=send_sems.at[index],
                        recv_sem=recv_sems.at[index],
                        device_id={"seq": lax.rem(chip + behind, chips) * 2 + to_core},
                        device_id_type=MESH,
                    )
                )
    return own, remote


def greet_halo(barrier, chips, reach, step):
    me = lax.axis_index("seq")
    chip = me // 2
    core = lax.rem(me, 2)
    for away in range(reach + 1):
        for cross in range(2):
            if away == 0 and cross == 0:
                continue
            to_core = core if cross == 0 else 1 - core
            peer = lax.rem(chip + chips + step * away, chips) * 2 + to_core
            pl.semaphore_signal(barrier, inc=1, device_id={"seq": peer}, device_id_type=MESH)


def gather_kernel(
    chips,
    depth,
    reach,
    q_ref,
    o_ref,
    k_ref,
    w_ref,
    qc_ref,
    oc_ref,
    kc_ref,
    wc_ref,
    halo_send,
    halo_recv,
    pair_send,
    pair_recv,
    local_sem,
    ring_send,
    ring_recv,
    hand_send,
    hand_recv,
):
    me = lax.axis_index("seq")
    layer = lax.axis_index("fsdp")
    core = lax.rem(me, 2)
    partner = me + 1 - 2 * core
    up = lax.rem(layer + 1, depth)
    down = lax.rem(layer + depth - 1, depth)

    barrier = pltpu.get_barrier_semaphore()
    greet_halo(barrier, chips, reach, -1)
    for peer in (up, down):
        pl.semaphore_signal(barrier, inc=1, device_id={"fsdp": peer}, device_id_type=MESH)
    pl.semaphore_wait(barrier, 2 * reach + 3)

    shard = w_ref.shape[0]
    half = shard // 2
    quarter = half // 2
    steps = depth // 2

    def ring_rows(block, step, way):
        first = block * shard + core * half
        if step < steps:
            return pl.ds(pl.multiple_of(first, half), half)
        return pl.ds(pl.multiple_of(first + way * quarter, quarter), quarter)

    def ring_copy(step, way):
        if way == 0:
            block, peer = lax.rem(layer + depth - (step - 1), depth), up
        else:
            block, peer = lax.rem(layer + (step - 1), depth), down
        rows = ring_rows(block, step, way)
        if step == 1:
            first = core * half
            source = w_ref.at[pl.ds(pl.multiple_of(first, half), half), :]
            rows = pl.ds(pl.multiple_of(block * shard + first, half), half)
        else:
            source = wc_ref.at[rows, :]
        return pltpu.make_async_remote_copy(
            src_ref=source,
            dst_ref=wc_ref.at[rows, :],
            send_sem=ring_send.at[way, step - 1],
            recv_sem=ring_recv.at[way, step - 1],
            device_id={"fsdp": peer},
            device_id_type=MESH,
        )

    def hand_copy(step, way, sender):
        block = lax.rem(layer + depth + (step if way else -step), depth)
        first = block * shard + sender * half
        if step < steps:
            rows = pl.ds(pl.multiple_of(first, half), half)
        else:
            rows = pl.ds(pl.multiple_of(first + way * quarter, quarter), quarter)
        return pltpu.make_async_remote_copy(
            src_ref=wc_ref.at[rows, :],
            dst_ref=wc_ref.at[rows, :],
            send_sem=hand_send.at[way, step - 1],
            recv_sem=hand_recv.at[way, step - 1],
            device_id={"seq": partner},
            device_id_type=MESH,
        )

    def got_copy(step, way):
        block = lax.rem(layer + depth + (step if way else -step), depth)
        rows = ring_rows(block, step, way)
        return pltpu.make_async_remote_copy(
            src_ref=wc_ref.at[rows, :],
            dst_ref=wc_ref.at[rows, :],
            send_sem=ring_send.at[way, step - 1],
            recv_sem=ring_recv.at[way, step - 1],
            device_id={"fsdp": up},
            device_id_type=MESH,
        )

    sent = []
    for way in range(2):
        copy = ring_copy(1, way)
        copy.start()
        sent.append(copy)

    own_key, keys = halo_copies(k_ref, kc_ref, halo_send, halo_recv, chips, reach)
    for copy in keys:
        copy.start()
    own_key.start()
    rows = q_ref.shape[0]
    wide = q_ref.shape[1] // 2
    here = pl.ds(pl.multiple_of(core * rows, rows), rows)
    mine = pl.ds(pl.multiple_of(core * wide, wide), wide)
    theirs = pl.ds(pl.multiple_of((1 - core) * wide, wide), wide)
    pairs = []
    locals_ = [own_key]
    for index, (source_ref, target_ref) in enumerate(((q_ref, qc_ref), (o_ref, oc_ref))):
        copy = pltpu.make_async_remote_copy(
            src_ref=source_ref.at[:, theirs],
            dst_ref=target_ref.at[here, :],
            send_sem=pair_send.at[index],
            recv_sem=pair_recv.at[index],
            device_id={"seq": partner},
            device_id_type=MESH,
        )
        copy.start()
        pairs.append(copy)
        copy = pltpu.make_async_copy(
            source_ref.at[:, mine], target_ref.at[here, :], local_sem.at[index]
        )
        copy.start()
        locals_.append(copy)
    copy = pltpu.make_async_copy(
        w_ref,
        wc_ref.at[pl.ds(pl.multiple_of(layer * shard, shard), shard), :],
        local_sem.at[2],
    )
    copy.start()
    locals_.append(copy)

    hands = []
    for step in range(1, steps + 1):
        for way in range(2):
            got_copy(step, way).wait_recv()
            if step < steps:
                copy = ring_copy(step + 1, way)
                copy.start()
                sent.append(copy)
            copy = hand_copy(step, way, core)
            copy.start()
            hands.append(copy)
    for copy in locals_:
        copy.wait()
    for copy in sent:
        copy.wait_send()
    for copy in hands:
        copy.wait_send()
    for step in range(1, steps + 1):
        for way in range(2):
            hand_copy(step, way, 1 - core).wait_recv()
    for copy in keys:
        copy.wait()
    for copy in pairs:
        copy.wait()


def gather_all(queries, grads, keys, weight, chips, depth, reach):
    rows, width = queries.shape
    kv = keys.shape[1]
    sems = pltpu.SemaphoreType.DMA
    links = 2 * (reach + 1)
    anywhere = pl.BlockSpec(memory_space=pl.ANY)
    vmem = pl.BlockSpec(memory_space=pltpu.VMEM)
    dtype = jnp.bfloat16
    return pl.pallas_call(
        functools.partial(gather_kernel, chips, depth, reach),
        out_shape=(
            jax.ShapeDtypeStruct((2 * rows, width // 2), dtype),
            jax.ShapeDtypeStruct((2 * rows, width // 2), dtype),
            jax.ShapeDtypeStruct((links * rows, kv // 2), dtype),
            jax.ShapeDtypeStruct((depth * weight.shape[0], weight.shape[1]), dtype),
        ),
        in_specs=[vmem] * 4,
        out_specs=(anywhere,) * 4,
        scratch_shapes=[
            sems((links,)),
            sems((links,)),
            sems((2,)),
            sems((2,)),
            sems((3,)),
            sems((2, depth // 2)),
            sems((2, depth // 2)),
            sems((2, depth // 2)),
            sems((2, depth // 2)),
        ],
        compiler_params=pltpu.CompilerParams(collective_id=1, has_side_effects=True),
        name="gather_inputs",
    )(queries, grads, keys, weight)


def halo_kernel(chips, reach, v_ref, vc_ref, send_sems, recv_sems):
    barrier = pltpu.get_barrier_semaphore()
    greet_halo(barrier, chips, reach, -1)
    pl.semaphore_wait(barrier, 2 * reach + 1)
    own, remote = halo_copies(v_ref, vc_ref, send_sems, recv_sems, chips, reach)
    for copy in remote:
        copy.start()
    own.start()
    own.wait()
    for copy in remote:
        copy.wait()


def gather_values(values, chips, reach):
    rows, kv = values.shape
    links = 2 * (reach + 1)
    sems = pltpu.SemaphoreType.DMA
    return pl.pallas_call(
        functools.partial(halo_kernel, chips, reach),
        out_shape=jax.ShapeDtypeStruct((links * rows, kv // 2), values.dtype),
        in_specs=[pl.BlockSpec(memory_space=pltpu.VMEM)],
        out_specs=pl.BlockSpec(memory_space=pl.ANY),
        scratch_shapes=[sems((links,)), sems((links,))],
        compiler_params=pltpu.CompilerParams(collective_id=2, has_side_effects=True),
        name="gather_values",
    )(values)


def attention_kernel(
    info_ref,
    q_ref,
    o_ref,
    k_ref,
    v_ref,
    dq_ref,
    dkv_ref,
    bias_ref,
    s_ref,
    g_ref,
    p_ref,
    d_ref,
    acc_ref,
):
    chip = info_ref[0]
    side = pl.program_id(1)
    rows = q_ref.shape[0]
    heads = q_ref.shape[1] // HEAD_FEATURES
    window = bias_ref.shape[0]
    span = k_ref.shape[0]
    start = pl.multiple_of(side * rows, rows)
    inverse = HEAD_FEATURES ** (-0.5)
    steep = inverse * LOG2_E
    chunk = 128
    count = window // chunk

    @pl.when(side == 0)
    def _():
        acc_ref[...] = jnp.zeros_like(acc_ref)

    q_place = chip * (2 * rows) + start + lax.broadcasted_iota(jnp.int32, (1, rows), 1)
    finish = jnp.int32(0)
    opening = jnp.zeros((1, rows), jnp.int32)
    for index in range(DOCS):
        finish = finish + info_ref[1 + index]
        opening = jnp.where(q_place >= finish, finish, opening)
    for part in range(count):
        k_place = (
            chip * (2 * rows)
            - (span - 2 * rows)
            + start
            + part * chunk
            + lax.broadcasted_iota(jnp.int32, (chunk, rows), 0)
        )
        allowed = (k_place >= opening) & (k_place <= q_place)
        bias_ref[part * chunk : (part + 1) * chunk, :] = jnp.where(allowed, 0.0, NEG_FILL)

    def stack(ref, first, number):
        return jnp.concatenate(
            [
                ref[:, (first + i) * HEAD_FEATURES : (first + i + 1) * HEAD_FEATURES]
                for i in range(number)
            ],
            axis=0,
        )

    def fold(values):
        return values.reshape(chunk // 8, 8, values.shape[1])

    trailing = (((1,), (1,)), ((), ()))
    for pair in range(heads // 2):
        q_pair = stack(q_ref, 2 * pair, 2)
        o_pair = stack(o_ref, 2 * pair, 2)
        lanes = slice(pair * 2 * rows, (pair + 1) * 2 * rows)
        peak = None
        for part in range(count):
            here = slice(part * chunk, (part + 1) * chunk)
            scores = lax.dot_general(
                k_ref[pl.ds(start + part * chunk, chunk), :],
                q_pair,
                trailing,
                preferred_element_type=jnp.float32,
            )
            bias = bias_ref[here, :]
            scores = scores + jnp.concatenate([bias, bias], axis=1)
            s_ref[here, :] = scores
            high = jnp.max(fold(scores), axis=0)
            peak = high if peak is None else jnp.maximum(peak, high)
        peak = jnp.max(peak, axis=0, keepdims=True)
        total = jnp.zeros((8, 2 * rows), jnp.float32)
        delta = jnp.zeros((8, 2 * rows), jnp.float32)
        for part in range(count):
            here = slice(part * chunk, (part + 1) * chunk)
            weights = jnp.exp2((s_ref[here, :] - peak) * steep)
            grad_probs = lax.dot_general(
                v_ref[pl.ds(start + part * chunk, chunk), :],
                o_pair,
                trailing,
                preferred_element_type=jnp.float32,
            )
            total = total + jnp.sum(fold(weights), axis=0)
            delta = delta + jnp.sum(fold(weights * grad_probs), axis=0)
            s_ref[here, :] = weights
            g_ref[here, :] = grad_probs
        scale = 1.0 / jnp.sum(total, axis=0, keepdims=True)
        delta = jnp.sum(delta, axis=0, keepdims=True) * scale
        for part in range(count):
            here = slice(part * chunk, (part + 1) * chunk)
            probs = s_ref[here, :] * scale
            p_ref[here, lanes] = probs.astype(jnp.bfloat16)
            d_ref[here, lanes] = (probs * (g_ref[here, :] - delta)).astype(jnp.bfloat16)

    rows_here = pl.ds(start, window)
    acc_ref[0, rows_here, :] += inverse * jnp.dot(
        d_ref[...], stack(q_ref, 0, heads), preferred_element_type=jnp.float32
    )
    acc_ref[1, rows_here, :] += jnp.dot(
        p_ref[...], stack(o_ref, 0, heads), preferred_element_type=jnp.float32
    )
    grad_t = lax.dot_general(
        k_ref[rows_here, :],
        d_ref[...],
        (((0,), (0,)), ((), ())),
        preferred_element_type=jnp.float32,
    )
    for head in range(heads):
        block = grad_t[:, head * rows : (head + 1) * rows]
        dq_ref[:, head * HEAD_FEATURES : (head + 1) * HEAD_FEATURES] = (
            block.T * inverse
        ).astype(jnp.bfloat16)

    @pl.when(side == 1)
    def _():
        dkv_ref[...] = acc_ref[...].astype(jnp.bfloat16)


def attend(info, queries, grads, keys, values):
    tokens, width = queries.shape
    rows = tokens // 2
    span, kv = keys.shape
    groups = kv // HEAD_FEATURES
    wide = width // groups
    window = span - rows
    stacked = rows * wide // HEAD_FEATURES
    query_spec = pl.BlockSpec((rows, wide), lambda group, side, info_ref: (side, group))
    key_spec = pl.BlockSpec((span, HEAD_FEATURES), lambda group, side, info_ref: (0, group))
    return pl.pallas_call(
        attention_kernel,
        grid_spec=pltpu.PrefetchScalarGridSpec(
            num_scalar_prefetch=1,
            grid=(groups, 2),
            in_specs=[query_spec, query_spec, key_spec, key_spec],
            out_specs=(
                query_spec,
                pl.BlockSpec(
                    (2, span, HEAD_FEATURES), lambda group, side, info_ref: (0, 0, group)
                ),
            ),
            scratch_shapes=[
                pltpu.VMEM((window, rows), jnp.float32),
                pltpu.VMEM((window, 2 * rows), jnp.float32),
                pltpu.VMEM((window, 2 * rows), jnp.float32),
                pltpu.VMEM((window, stacked), jnp.bfloat16),
                pltpu.VMEM((window, stacked), jnp.bfloat16),
                pltpu.VMEM((2, span, HEAD_FEATURES), jnp.float32),
            ],
        ),
        out_shape=(
            jax.ShapeDtypeStruct((tokens, width), jnp.bfloat16),
            jax.ShapeDtypeStruct((2, span, kv), jnp.bfloat16),
        ),
        name="attention_backward",
    )(info, queries, grads, keys, values)


def return_kernel(
    chips, reach, dq_ref, dkv_ref, full_ref, parts_ref, send_sems, recv_sems, pair_send, pair_recv, local_sem
):
    me = lax.axis_index("seq")
    chip = me // 2
    core = lax.rem(me, 2)
    partner = me + 1 - 2 * core
    barrier = pltpu.get_barrier_semaphore()
    greet_halo(barrier, chips, reach, 1)
    pl.semaphore_wait(barrier, 2 * reach + 1)

    rows = full_ref.shape[0]
    wide = dq_ref.shape[1]
    half = dkv_ref.shape[2]
    kv_lanes = pl.ds(pl.multiple_of(core * half, half), half)
    waits = []
    for behind in range(reach, -1, -1):
        for cross in range(2):
            to_core = core if cross == 0 else 1 - core
            slot = pl.multiple_of(((reach - behind) * 2 + to_core) * rows, rows)
            source = dkv_ref.at[:, pl.ds(slot, rows), :]
            target = parts_ref.at[behind, :, :, kv_lanes]
            index = behind * 2 + cross
            if index == 0:
                copy = pltpu.make_async_copy(source, target, local_sem.at[0])
            else:
                copy = pltpu.make_async_remote_copy(
                    src_ref=source,
                    dst_ref=target,
                    send_sem=send_sems.at[index],
                    recv_sem=recv_sems.at[index],
                    device_id={"seq": lax.rem(chip + chips - behind, chips) * 2 + to_core},
                    device_id_type=MESH,
                )
            copy.start()
            waits.append(copy)
    lanes = pl.ds(pl.multiple_of(core * wide, wide), wide)
    copy = pltpu.make_async_remote_copy(
        src_ref=dq_ref.at[pl.ds(pl.multiple_of((1 - core) * rows, rows), rows), :],
        dst_ref=full_ref.at[:, lanes],
        send_sem=pair_send,
        recv_sem=pair_recv,
        device_id={"seq": partner},
        device_id_type=MESH,
    )
    copy.start()
    waits.append(copy)
    copy = pltpu.make_async_copy(
        dq_ref.at[pl.ds(pl.multiple_of(core * rows, rows), rows), :],
        full_ref.at[:, lanes],
        local_sem.at[1],
    )
    copy.start()
    waits.append(copy)
    for copy in waits:
        copy.wait()


def give_back(grad_queries, grad_pairs, chips, reach):
    tokens, width = grad_queries.shape
    kv = grad_pairs.shape[2]
    rows = tokens // 2
    links = 2 * (reach + 1)
    sems = pltpu.SemaphoreType.DMA
    anywhere = pl.BlockSpec(memory_space=pl.ANY)
    vmem = pl.BlockSpec(memory_space=pltpu.VMEM)
    return pl.pallas_call(
        functools.partial(return_kernel, chips, reach),
        out_shape=(
            jax.ShapeDtypeStruct((rows, 2 * width), jnp.bfloat16),
            jax.ShapeDtypeStruct((reach + 1, 2, rows, 2 * kv), jnp.bfloat16),
        ),
        in_specs=[vmem, vmem],
        out_specs=(anywhere, anywhere),
        scratch_shapes=[sems((links,)), sems((links,)), sems, sems, sems((2,))],
        compiler_params=pltpu.CompilerParams(collective_id=3, has_side_effects=True),
        name="return_gradients",
    )(grad_queries, grad_pairs)


def contract_trailing(left_rows, right_rows):
    return lax.dot_general(
        left_rows, right_rows, (((1,), (1,)), ((), ())), preferred_element_type=jnp.float32
    )


def body(
    normed_block_input,
    stored_rotated_queries,
    stored_rotated_keys,
    attention_output_gradient,
    frozen_value_weight,
    adapter_down_weight,
    adapter_up_weight,
    packed_document_lengths,
):
    token_rows = normed_block_input.shape[1]
    model_features = normed_block_input.shape[2]
    hidden_activations = normed_block_input.reshape(token_rows, model_features)
    seq_count = lax.axis_size("seq")
    fsdp_count = lax.axis_size("fsdp")
    chips = seq_count // 2
    reach = DOC_MOST // (2 * token_rows)
    up_widened = adapter_up_weight.astype(jnp.float32)

    queries, grads, keys, weight = gather_all(
        stored_rotated_queries[0],
        attention_output_gradient[0],
        stored_rotated_keys[0],
        frozen_value_weight,
        chips,
        fsdp_count,
        reach,
    )
    adapter_projection = contract_trailing(hidden_activations, adapter_down_weight)
    adapter_maps = ADAPTER_SCALE * jnp.dot(
        adapter_projection, up_widened, precision=lax.Precision.HIGHEST
    )
    base_value = jnp.dot(hidden_activations, weight, preferred_element_type=jnp.float32)
    adapter_values = (base_value + adapter_maps).astype(jnp.bfloat16)
    values = gather_values(adapter_values, chips, reach)
    info = jnp.concatenate(
        [(lax.axis_index("seq") // 2).astype(jnp.int32)[None], packed_document_lengths[0]]
    )
    grad_queries, grad_pairs = attend(info, queries, grads, keys, values)
    rotated_query_gradient, parts = give_back(grad_queries, grad_pairs, chips, reach)
    summed = parts.astype(jnp.float32).sum(axis=0)
    rotated_key_gradient = summed[0].astype(jnp.bfloat16)
    value_gradient_matrix = summed[1]
    value_grad_low = value_gradient_matrix.astype(jnp.bfloat16)
    adapter_rank_gradient = ADAPTER_SCALE * lax.dot_general(
        value_gradient_matrix, up_widened, (((1,), (1,)), ((), ())), precision=lax.Precision.HIGHEST
    )
    reduced_rank_gradient = adapter_rank_gradient.astype(jnp.bfloat16)
    overall_token_count = token_rows * seq_count * fsdp_count
    down_shard = (
        lax.dot_general(
            reduced_rank_gradient,
            hidden_activations,
            (((0,), (0,)), ((), ())),
            preferred_element_type=jnp.float32,
        )
        / overall_token_count
    )
    up_shard = (
        ADAPTER_SCALE
        * jnp.dot(adapter_projection.T, value_gradient_matrix, precision=lax.Precision.HIGHEST)
        / overall_token_count
    )
    adapter_down_gradient, adapter_up_gradient = sum_over_mesh(
        down_shard, up_shard, seq_count, fsdp_count
    )
    frozen_path_gradient = contract_trailing(value_grad_low, weight)
    input_gradient = (
        frozen_path_gradient
        + jnp.dot(reduced_rank_gradient, adapter_down_weight, preferred_element_type=jnp.float32)
    ).astype(jnp.bfloat16)
    return (
        input_gradient[None],
        rotated_query_gradient[None],
        rotated_key_gradient[None],
        adapter_down_gradient,
        adapter_up_gradient,
    )


def solution(mesh):
    placed = (
        P("fsdp", "seq", None),
        P("fsdp", "seq", None),
        P("fsdp", "seq", None),
        P("fsdp", "seq", None),
        P("fsdp", None),
        P(),
        P(),
        P("fsdp", None),
    )
    return jax.shard_map(
        body,
        mesh=mesh,
        in_specs=placed,
        out_specs=(
            P("fsdp", "seq", None),
            P("fsdp", "seq", None),
            P("fsdp", "seq", None),
            P(),
            P(),
        ),
        check_vma=False,
    )
```

```python
import functools

import jax
import jax.numpy as jnp
from jax import lax
from jax.experimental import pallas as pl
from jax.experimental.pallas import tpu as pltpu
from jax.sharding import PartitionSpec as P

HEAD_FEATURES = 128


ADAPTER_SCALE = 2.0
NEG_FILL = -1e30
LOG2_E = 1.4426950408889634
DOCS = 8
DOC_MOST = 1024


MESH = pl.DeviceIdType.MESH
SUM_LANES = 256
SUM_WIDE = 384


def sum_kernel(
    chips,
    depth,
    down_ref,
    up_ref,
    grad_ref,
    rank_ref,
    map_ref,
    weight_ref,
    down_out,
    up_out,
    input_out,
    parts_ref,
    pair_in,
    pair_total,
    chip_in,
    depth_in,
    final_ref,
    weight_in,
    weight_sems,
    pair_send,
    pair_recv,
    chip_send,
    chip_recv,
    depth_send,
    depth_recv,
    give_send,
    give_recv,
    hand_send,
    hand_recv,
):
    me = lax.axis_index("seq")
    layer = lax.axis_index("fsdp")
    chip = me // 2
    core = lax.rem(me, 2)
    partner = chip * 2 + 1 - core
    tiles = weight_sems.shape[0]
    tile = weight_ref.shape[0] // tiles

    def chip_peer(offset):
        return lax.rem(chip + offset, chips) * 2 + core

    def depth_peer(offset):
        return lax.rem(layer + offset, depth)

    def weight_copy(index):
        rows = pl.ds(pl.multiple_of(index * tile, tile), tile)
        return pltpu.make_async_copy(
            weight_ref.at[rows, :], weight_in.at[rows, :], weight_sems.at[index]
        )

    for index in range(tiles):
        weight_copy(index).start()

    barrier = pltpu.get_barrier_semaphore()
    pl.semaphore_signal(barrier, inc=1, device_id={"seq": partner}, device_id_type=MESH)
    for offset in range(1, chips):
        pl.semaphore_signal(
            barrier, inc=1, device_id={"seq": chip_peer(offset)}, device_id_type=MESH
        )
    for offset in range(1, depth):
        pl.semaphore_signal(
            barrier, inc=1, device_id={"fsdp": depth_peer(offset)}, device_id_type=MESH
        )

    spare = up_ref.shape[1] // 128
    parts_ref[:, :, :, SUM_LANES:] = jnp.zeros_like(parts_ref[:, :, :, SUM_LANES:])
    for index in range(spare):
        parts_ref[index // 2, index % 2, :, SUM_LANES:] = up_ref[
            :, index * 128 : (index + 1) * 128
        ]
    for index in range(2 * chips):
        parts_ref[index // 2, index % 2, :, :SUM_LANES] = down_ref[
            :, index * SUM_LANES : (index + 1) * SUM_LANES
        ]
    pl.semaphore_wait(barrier, chips + depth - 1)

    pair = pltpu.make_async_remote_copy(
        src_ref=parts_ref.at[:, 1 - core],
        dst_ref=pair_in,
        send_sem=pair_send,
        recv_sem=pair_recv,
        device_id={"seq": partner},
        device_id_type=MESH,
    )
    pair.start()
    pair.wait()

    def add_pair(index, carry):
        pair_total[index] = (parts_ref[index, core] + pair_in[index]).astype(jnp.bfloat16)
        return carry

    lax.fori_loop(0, chips, add_pair, 0)

    copies = []
    for offset in range(1, chips):
        target = lax.rem(chip + offset, chips)
        copy = pltpu.make_async_remote_copy(
            src_ref=pair_total.at[target],
            dst_ref=chip_in.at[offset - 1],
            send_sem=chip_send.at[offset - 1],
            recv_sem=chip_recv.at[offset - 1],
            device_id={"seq": chip_peer(offset)},
            device_id_type=MESH,
        )
        copy.start()
        copies.append(copy)

    def project(index, carry):
        weight_copy(index).wait()
        lanes = pl.ds(pl.multiple_of(index * tile, tile), tile)
        gradient = lax.dot_general(
            grad_ref[...],
            weight_in[lanes, :],
            (((1,), (1,)), ((), ())),
            preferred_element_type=jnp.float32,
        ) + jnp.dot(rank_ref[...], map_ref[:, lanes], preferred_element_type=jnp.float32)
        input_out[:, lanes] = gradient.astype(jnp.bfloat16)
        return carry

    lax.fori_loop(0, tiles, project, 0)

    for copy in copies:
        copy.wait()
    total = pair_total[chip].astype(jnp.float32)
    for offset in range(chips - 1):
        total = total + chip_in[offset].astype(jnp.float32)
    depth_in[layer] = total.astype(jnp.bfloat16)

    copies = []
    for offset in range(1, depth):
        copies.append(
            pltpu.make_async_remote_copy(
                src_ref=depth_in.at[layer],
                dst_ref=depth_in.at[layer],
                send_sem=depth_send.at[offset - 1],
                recv_sem=depth_recv.at[offset - 1],
                device_id={"fsdp": depth_peer(offset)},
                device_id_type=MESH,
            )
        )
    for copy in copies:
        copy.start()
    for offset, copy in enumerate(copies, 1):
        source = lax.rem(layer + depth - offset, depth)
        copy.wait_send()
        pltpu.make_async_remote_copy(
            src_ref=depth_in.at[source],
            dst_ref=depth_in.at[source],
            send_sem=depth_send.at[offset - 1],
            recv_sem=depth_recv.at[offset - 1],
            device_id={"fsdp": depth_peer(offset)},
            device_id_type=MESH,
        ).wait_recv()
    final = depth_in[0].astype(jnp.float32)
    for index in range(1, depth):
        final = final + depth_in[index].astype(jnp.float32)
    final_ref[chip, core] = final.astype(jnp.bfloat16)

    gives = []
    for offset in range(1, chips):
        copy = pltpu.make_async_remote_copy(
            src_ref=final_ref.at[chip, core],
            dst_ref=final_ref.at[chip, core],
            send_sem=give_send.at[offset - 1],
            recv_sem=give_recv.at[offset - 1],
            device_id={"seq": chip_peer(offset)},
            device_id_type=MESH,
        )
        copy.start()
        gives.append(copy)

    def hand_copy(offset, sender):
        owner = lax.rem(chip + chips - offset, chips)
        return pltpu.make_async_remote_copy(
            src_ref=final_ref.at[owner, sender],
            dst_ref=final_ref.at[owner, sender],
            send_sem=hand_send.at[offset],
            recv_sem=hand_recv.at[offset],
            device_id={"seq": partner},
            device_id_type=MESH,
        )

    hands = []
    for offset in range(chips):
        if offset:
            owner = lax.rem(chip + chips - offset, chips)
            pltpu.make_async_remote_copy(
                src_ref=final_ref.at[owner, core],
                dst_ref=final_ref.at[owner, core],
                send_sem=give_send.at[offset - 1],
                recv_sem=give_recv.at[offset - 1],
                device_id={"seq": chip_peer(offset)},
                device_id_type=MESH,
            ).wait_recv()
        hand = hand_copy(offset, core)
        hand.start()
        hands.append(hand)
    for copy in gives:
        copy.wait_send()
    for offset, hand in enumerate(hands):
        hand.wait_send()
        hand_copy(offset, 1 - core).wait_recv()
    for index in range(2 * chips):
        down_out[:, index * SUM_LANES : (index + 1) * SUM_LANES] = final_ref[
            index // 2, index % 2, :, :SUM_LANES
        ].astype(jnp.float32)
    for index in range(spare):
        up_out[:, index * 128 : (index + 1) * 128] = final_ref[
            index // 2, index % 2, :, SUM_LANES:
        ].astype(jnp.float32)


def sum_over_mesh(
    down_shard, up_shard, value_grad, rank_grad, down_weight, weight, seq_count, fsdp_count
):
    chips = seq_count // 2
    rank = down_shard.shape[0]
    block = (rank, SUM_WIDE)
    tiles = 8
    sems = pltpu.SemaphoreType.DMA
    vmem = pl.BlockSpec(memory_space=pltpu.VMEM)
    return pl.pallas_call(
        functools.partial(sum_kernel, chips, fsdp_count),
        out_shape=(
            jax.ShapeDtypeStruct(down_shard.shape, jnp.float32),
            jax.ShapeDtypeStruct(up_shard.shape, jnp.float32),
            jax.ShapeDtypeStruct((value_grad.shape[0], weight.shape[0]), jnp.bfloat16),
        ),
        in_specs=[vmem] * 5 + [pl.BlockSpec(memory_space=pl.ANY)],
        out_specs=(vmem,) * 3,
        scratch_shapes=[
            pltpu.VMEM((chips, 2) + block, jnp.float32),
            pltpu.VMEM((chips,) + block, jnp.float32),
            pltpu.VMEM((chips,) + block, jnp.bfloat16),
            pltpu.VMEM((chips - 1,) + block, jnp.bfloat16),
            pltpu.VMEM((fsdp_count,) + block, jnp.bfloat16),
            pltpu.VMEM((chips, 2) + block, jnp.bfloat16),
            pltpu.VMEM(weight.shape, jnp.bfloat16),
            sems((tiles,)),
            sems,
            sems,
            sems((chips - 1,)),
            sems((chips - 1,)),
            sems((fsdp_count - 1,)),
            sems((fsdp_count - 1,)),
            sems((chips - 1,)),
            sems((chips - 1,)),
            sems((chips,)),
            sems((chips,)),
        ],
        compiler_params=pltpu.CompilerParams(collective_id=0, has_side_effects=True),
        name="adapter_sum",
    )(down_shard, up_shard, value_grad, rank_grad, down_weight, weight)


SIDE = 4


class Place:
    def __init__(self):
        me = lax.axis_index("seq")
        self.chip = me // 2
        self.core = lax.rem(me, 2)
        self.column = lax.rem(self.chip, SIDE)
        self.row = self.chip // SIDE
        self.partner = me + 1 - 2 * self.core

    def along_x(self, offset):
        column = lax.rem(self.column + offset + SIDE, SIDE)
        return (self.row * SIDE + column) * 2 + self.core

    def along_y(self, offset):
        row = lax.rem(self.row + offset + SIDE, SIDE)
        return (row * SIDE + self.column) * 2 + self.core

    def greet(self, barrier):
        peers = [self.partner] + [self.along_x(i) for i in range(1, SIDE)]
        peers += [self.along_y(1), self.along_y(-1)]
        for peer in peers:
            pl.semaphore_signal(barrier, inc=1, device_id={"seq": peer}, device_id_type=MESH)
        return len(peers)


class Halo:
    LINKS = SIDE + 2

    def __init__(self, place, source_ref, target_ref, send_sems, recv_sems, local_sem):
        self.place = place
        self.target_ref = target_ref
        self.send_sems, self.recv_sems = send_sems, recv_sems
        rows, width = source_ref.shape
        half = width // 2
        self.block = 2 * rows
        core = place.core
        first = SIDE * self.block + core * rows
        here = target_ref.at[pl.ds(pl.multiple_of(first, rows), rows), :]
        mine = pl.ds(pl.multiple_of(core * half, half), half)
        theirs = pl.ds(pl.multiple_of((1 - core) * half, half), half)
        self.own = pltpu.make_async_copy(source_ref.at[:, mine], here, local_sem)
        self.pair = pltpu.make_async_remote_copy(
            src_ref=source_ref.at[:, theirs],
            dst_ref=here,
            send_sem=send_sems.at[0],
            recv_sem=recv_sems.at[0],
            device_id={"seq": place.partner},
            device_id_type=MESH,
        )

    def copy(self, index, source, target, peer):
        first = source * self.block
        return pltpu.make_async_remote_copy(
            src_ref=self.target_ref.at[
                pl.ds(pl.multiple_of(first, self.block), self.block), :
            ],
            dst_ref=self.target_ref.at[pl.ds(target * self.block, self.block), :],
            send_sem=self.send_sems.at[index],
            recv_sem=self.recv_sems.at[index],
            device_id={"seq": peer},
            device_id_type=MESH,
        )

    def start(self):
        self.own.start()
        self.pair.start()

    def along_x(self, offset):
        wraps = (self.place.column + offset) // SIDE
        index = 2 if offset == 1 else 3
        copy = self.copy(
            index, SIDE * (1 - wraps), SIDE - offset, self.place.along_x(offset)
        )
        return wraps, copy

    def spread(self):
        place = self.place
        self.own.wait()
        self.pair.wait()
        self.vertical = self.copy(1, SIDE, 0, place.along_y(1))
        self.vertical.start()
        self.sideways = [self.along_x(1), self.along_x(SIDE - 1)]
        for wraps, copy in self.sideways:

            @pl.when(wraps == 0)
            def _():
                copy.start()

        self.vertical.wait_recv()
        for wraps, copy in self.sideways:

            @pl.when(wraps == 1)
            def _():
                copy.start()

    def relay(self):
        place = self.place
        inner = (place.column == 1) | (place.column == 2)
        self.sideways[0][1].wait_recv()
        forward = self.copy(4, SIDE - 1, SIDE - 2, place.along_x(1))

        @pl.when(inner)
        def _():
            forward.start()

        self.sideways[1][1].wait_recv()
        backward = self.copy(5, 1, SIDE - 2, place.along_x(-1))

        @pl.when(inner)
        def _():
            backward.start()

        self.relays = (inner, forward, backward)

    def finish(self):
        inner, forward, backward = self.relays
        left = self.place.column < SIDE // 2

        @pl.when(left)
        def _():
            backward.wait_recv()

        @pl.when(jnp.logical_not(left))
        def _():
            forward.wait_recv()

        @pl.when(inner)
        def _():
            forward.wait_send()
            backward.wait_send()

        self.vertical.wait_send()
        for _, copy in self.sideways:
            copy.wait_send()


RING_ROWS = 256
SLICE_ROWS = 48


def gather_kernel(
    depth,
    q_ref,
    o_ref,
    k_ref,
    w_ref,
    qc_ref,
    oc_ref,
    kc_ref,
    wc_ref,
    halo_send,
    halo_recv,
    pair_send,
    pair_recv,
    local_sem,
    ring_send,
    ring_recv,
    hand_send,
    hand_recv,
    deep_send,
    deep_recv,
    plane_send,
    plane_recv,
    pass_send,
    pass_recv,
):
    place = Place()
    core, partner = place.core, place.partner
    layer = lax.axis_index("fsdp")
    up = lax.rem(layer + 1, depth)
    down = lax.rem(layer + depth - 1, depth)

    barrier = pltpu.get_barrier_semaphore()
    count = place.greet(barrier)
    for peer in (up, down):
        pl.semaphore_signal(barrier, inc=1, device_id={"fsdp": peer}, device_id_type=MESH)
    pl.semaphore_wait(barrier, count + 2)

    shard = w_ref.shape[0]
    half = RING_ROWS // 2
    quarter = half // 2
    steps = depth // 2
    group = SIDE * SLICE_ROWS
    position = (place.column, place.row)

    def block_at(step, way):
        return lax.rem(layer + depth + (step if way else -step), depth)

    def remote(rows, source_rows, send, recv, peer, source_ref=None):
        return pltpu.make_async_remote_copy(
            src_ref=(wc_ref if source_ref is None else source_ref).at[source_rows, :],
            dst_ref=wc_ref.at[rows, :],
            send_sem=send,
            recv_sem=recv,
            device_id=peer,
            device_id_type=MESH,
        )

    def ring_rows(block, step, way, owner):
        first = block * shard + owner * half
        if step < steps:
            return pl.ds(pl.multiple_of(first, half), half)
        return pl.ds(pl.multiple_of(first + way * quarter, quarter), quarter)

    def slice_rows(block, axis, owner, spot):
        first = block * shard + RING_ROWS + axis * 2 * group + owner * group + spot * SLICE_ROWS
        return pl.ds(pl.multiple_of(first, 16), SLICE_ROWS)

    def group_rows(block, axis, owner):
        first = block * shard + RING_ROWS + axis * 2 * group + owner * group
        return pl.ds(pl.multiple_of(first, 16), group)

    def ring_copy(step, way):
        rows = ring_rows(block_at(step - 1, way), step, way, core)
        peer = {"fsdp": down if way else up}
        sems = ring_send.at[way, step - 1], ring_recv.at[way, step - 1]
        if step == 1:
            source = ring_rows(0, step, way, core)
            return remote(rows, source, *sems, peer, w_ref)
        return remote(rows, rows, *sems, peer)

    def ring_got(step, way):
        rows = ring_rows(block_at(step, way), step, way, core)
        sems = ring_send.at[way, step - 1], ring_recv.at[way, step - 1]
        return remote(rows, rows, *sems, {"fsdp": up})

    def ring_hand(step, way, owner):
        rows = ring_rows(block_at(step, way), step, way, owner)
        sems = hand_send.at[way, step - 1], hand_recv.at[way, step - 1]
        return remote(rows, rows, *sems, {"seq": partner})

    def deep_copy(step, way, axis):
        rows = slice_rows(block_at(step - 1, way), axis, core, position[axis])
        peer = {"fsdp": down if way else up}
        sems = deep_send.at[way, step - 1, axis], deep_recv.at[way, step - 1, axis]
        if step == 1:
            source = slice_rows(0, axis, core, position[axis])
            return remote(rows, source, *sems, peer, w_ref)
        return remote(rows, rows, *sems, peer)

    def deep_got(step, way, axis):
        rows = slice_rows(block_at(step, way), axis, core, position[axis])
        sems = deep_send.at[way, step - 1, axis], deep_recv.at[way, step - 1, axis]
        return remote(rows, rows, *sems, {"fsdp": up})

    def toward(axis, offset):
        return {"seq": place.along_y(offset) if axis else place.along_x(offset)}

    def plane_copy(number, block, axis, kind, sending):
        step_forward = 1 if kind == 0 or (kind == 2 and number % 2) else -1
        if kind == 2:
            spot = -1 if step_forward == 1 else 1
            if not sending:
                spot = 2
        else:
            spot = 0 if sending else -step_forward
        spot = lax.rem(position[axis] + spot + SIDE, SIDE)
        rows = slice_rows(block, axis, core, spot)
        sems = plane_send.at[axis, number - 1, kind], plane_recv.at[axis, number - 1, kind]
        return remote(rows, rows, *sems, toward(axis, step_forward))

    def pass_copy(number, block, axis, owner):
        rows = group_rows(block, axis, owner)
        sems = pass_send.at[axis, number - 1], pass_recv.at[axis, number - 1]
        return remote(rows, rows, *sems, {"seq": partner})

    sent = []

    def go(copy):
        copy.start()
        sent.append(copy)

    halo = Halo(place, k_ref, kc_ref, halo_send, halo_recv, local_sem.at[3])
    halo.start()
    for way in range(2):
        for axis in range(2):
            go(deep_copy(1, way, axis))
    for way in range(2):
        go(ring_copy(1, way))
    rows = q_ref.shape[0]
    wide = q_ref.shape[1] // 2
    here = pl.ds(pl.multiple_of(core * rows, rows), rows)
    mine = pl.ds(pl.multiple_of(core * wide, wide), wide)
    theirs = pl.ds(pl.multiple_of((1 - core) * wide, wide), wide)
    pairs = []
    locals_ = []
    for index, (source_ref, target_ref) in enumerate(((q_ref, qc_ref), (o_ref, oc_ref))):
        copy = pltpu.make_async_remote_copy(
            src_ref=source_ref.at[:, theirs],
            dst_ref=target_ref.at[here, :],
            send_sem=pair_send.at[index],
            recv_sem=pair_recv.at[index],
            device_id={"seq": partner},
            device_id_type=MESH,
        )
        copy.start()
        pairs.append(copy)
        copy = pltpu.make_async_copy(
            source_ref.at[:, mine], target_ref.at[here, :], local_sem.at[index]
        )
        copy.start()
        locals_.append(copy)
    copy = pltpu.make_async_copy(
        w_ref,
        wc_ref.at[pl.ds(pl.multiple_of(layer * shard, shard), shard), :],
        local_sem.at[2],
    )
    copy.start()
    locals_.append(copy)
    halo.spread()

    numbers = 2 * steps - 1
    blocks = {}
    for number in range(1, numbers + 1):
        step, way = (number + 1) // 2, (number - 1) % 2
        blocks[number] = block_at(step, way)

    def pass_on(number):
        for axis in range(2):
            plane_copy(number, blocks[number], axis, 0 if number % 2 else 1, False).wait_recv()
            go(plane_copy(number, blocks[number], axis, 2, True))

    def hand_over(number):
        for axis in range(2):
            plane_copy(number, blocks[number], axis, 1 if number % 2 else 0, False).wait_recv()
            plane_copy(number, blocks[number], axis, 2, False).wait_recv()
            go(pass_copy(number, blocks[number], axis, core))

    def ring_step(step):
        for way in range(2):
            ring_got(step, way).wait_recv()
            if step < steps:
                go(ring_copy(step + 1, way))
            go(ring_hand(step, way, core))

    for number in range(1, numbers + 1):
        step, way = (number + 1) // 2, (number - 1) % 2
        for axis in range(2):
            came = axis if step == steps else way
            deep_got(step, came, axis).wait_recv()
            if step + 1 < steps or (step + 1 == steps and axis == way):
                go(deep_copy(step + 1, way, axis))
            for kind in range(2):
                go(plane_copy(number, blocks[number], axis, kind, True))
        if number == 1:
            halo.relay()
        if number > 1:
            pass_on(number - 1)
        if number > 2:
            hand_over(number - 2)
        if number % 2 == 0:
            ring_step(number // 2)
    pass_on(numbers)
    hand_over(numbers - 1)
    ring_step(steps)
    hand_over(numbers)

    halo.finish()
    for copy in locals_:
        copy.wait()
    for copy in pairs:
        copy.wait()
    for copy in sent:
        copy.wait_send()
    for number in range(1, numbers + 1):
        for axis in range(2):
            pass_copy(number, blocks[number], axis, 1 - core).wait_recv()
    for step in range(1, steps + 1):
        for way in range(2):
            ring_hand(step, way, 1 - core).wait_recv()


def gather_all(queries, grads, keys, weight, depth):
    rows, width = queries.shape
    kv = keys.shape[1]
    sems = pltpu.SemaphoreType.DMA
    steps = depth // 2
    numbers = 2 * steps - 1
    anywhere = pl.BlockSpec(memory_space=pl.ANY)
    vmem = pl.BlockSpec(memory_space=pltpu.VMEM)
    dtype = jnp.bfloat16
    return pl.pallas_call(
        functools.partial(gather_kernel, depth),
        out_shape=(
            jax.ShapeDtypeStruct((2 * rows, width // 2), dtype),
            jax.ShapeDtypeStruct((2 * rows, width // 2), dtype),
            jax.ShapeDtypeStruct(((SIDE + 1) * 2 * rows, kv // 2), dtype),
            jax.ShapeDtypeStruct((depth * weight.shape[0], weight.shape[1]), dtype),
        ),
        in_specs=[vmem] * 4,
        out_specs=(anywhere,) * 4,
        scratch_shapes=[
            sems((Halo.LINKS,)),
            sems((Halo.LINKS,)),
            sems((2,)),
            sems((2,)),
            sems((4,)),
            sems((2, steps)),
            sems((2, steps)),
            sems((2, steps)),
            sems((2, steps)),
            sems((2, steps, 2)),
            sems((2, steps, 2)),
            sems((2, numbers, 3)),
            sems((2, numbers, 3)),
            sems((2, numbers)),
            sems((2, numbers)),
        ],
        compiler_params=pltpu.CompilerParams(collective_id=1, has_side_effects=True),
        name="gather_inputs",
    )(queries, grads, keys, weight)


def halo_kernel(v_ref, vc_ref, send_sems, recv_sems, local_sem):
    place = Place()
    barrier = pltpu.get_barrier_semaphore()
    count = place.greet(barrier)
    pl.semaphore_wait(barrier, count)
    halo = Halo(place, v_ref, vc_ref, send_sems, recv_sems, local_sem)
    halo.start()
    halo.spread()
    halo.relay()
    halo.finish()


def gather_values(values):
    rows, kv = values.shape
    sems = pltpu.SemaphoreType.DMA
    return pl.pallas_call(
        halo_kernel,
        out_shape=jax.ShapeDtypeStruct(((SIDE + 1) * 2 * rows, kv // 2), values.dtype),
        in_specs=[pl.BlockSpec(memory_space=pltpu.VMEM)],
        out_specs=pl.BlockSpec(memory_space=pl.ANY),
        scratch_shapes=[sems((Halo.LINKS,)), sems((Halo.LINKS,)), sems],
        compiler_params=pltpu.CompilerParams(collective_id=2, has_side_effects=True),
        name="gather_values",
    )(values)


def greet_halo(barrier, chips, reach, step):
    me = lax.axis_index("seq")
    chip = me // 2
    core = lax.rem(me, 2)
    for away in range(reach + 1):
        for cross in range(2):
            if away == 0 and cross == 0:
                continue
            to_core = core if cross == 0 else 1 - core
            peer = lax.rem(chip + chips + step * away, chips) * 2 + to_core
            pl.semaphore_signal(barrier, inc=1, device_id={"seq": peer}, device_id_type=MESH)


def attention_kernel(
    info_ref,
    q_ref,
    o_ref,
    k_ref,
    v_ref,
    dq_ref,
    dkv_ref,
    bias_ref,
    s_ref,
    g_ref,
    p_ref,
    d_ref,
    acc_ref,
):
    chip = info_ref[0]
    side = pl.program_id(1)
    rows = q_ref.shape[0]
    heads = q_ref.shape[1] // HEAD_FEATURES
    window = bias_ref.shape[0]
    span = k_ref.shape[0]
    start = pl.multiple_of(side * rows, rows)
    inverse = HEAD_FEATURES ** (-0.5)
    steep = inverse * LOG2_E
    chunk = 128
    count = window // chunk

    @pl.when(side == 0)
    def _():
        acc_ref[...] = jnp.zeros_like(acc_ref)

    q_place = chip * (2 * rows) + start + lax.broadcasted_iota(jnp.int32, (1, rows), 1)
    finish = jnp.int32(0)
    opening = jnp.zeros((1, rows), jnp.int32)
    for index in range(DOCS):
        finish = finish + info_ref[1 + index]
        opening = jnp.where(q_place >= finish, finish, opening)
    for part in range(count):
        k_place = (
            chip * (2 * rows)
            - (span - 2 * rows)
            + start
            + part * chunk
            + lax.broadcasted_iota(jnp.int32, (chunk, rows), 0)
        )
        allowed = (k_place >= opening) & (k_place <= q_place)
        bias_ref[part * chunk : (part + 1) * chunk, :] = jnp.where(allowed, 0.0, NEG_FILL)

    def stack(ref, first, number):
        return jnp.concatenate(
            [
                ref[:, (first + i) * HEAD_FEATURES : (first + i + 1) * HEAD_FEATURES]
                for i in range(number)
            ],
            axis=0,
        )

    def fold(values):
        return values.reshape(chunk // 8, 8, values.shape[1])

    trailing = (((1,), (1,)), ((), ()))
    for pair in range(heads // 2):
        q_pair = stack(q_ref, 2 * pair, 2)
        o_pair = stack(o_ref, 2 * pair, 2)
        lanes = slice(pair * 2 * rows, (pair + 1) * 2 * rows)
        peak = None
        for part in range(count):
            here = slice(part * chunk, (part + 1) * chunk)
            scores = lax.dot_general(
                k_ref[pl.ds(start + part * chunk, chunk), :],
                q_pair,
                trailing,
                preferred_element_type=jnp.float32,
            )
            bias = bias_ref[here, :]
            scores = scores + jnp.concatenate([bias, bias], axis=1)
            s_ref[here, :] = scores
            high = jnp.max(fold(scores), axis=0)
            peak = high if peak is None else jnp.maximum(peak, high)
        peak = jnp.max(peak, axis=0, keepdims=True)
        total = jnp.zeros((8, 2 * rows), jnp.float32)
        delta = jnp.zeros((8, 2 * rows), jnp.float32)
        for part in range(count):
            here = slice(part * chunk, (part + 1) * chunk)
            weights = jnp.exp2((s_ref[here, :] - peak) * steep)
            grad_probs = lax.dot_general(
                v_ref[pl.ds(start + part * chunk, chunk), :],
                o_pair,
                trailing,
                preferred_element_type=jnp.float32,
            )
            total = total + jnp.sum(fold(weights), axis=0)
            delta = delta + jnp.sum(fold(weights * grad_probs), axis=0)
            s_ref[here, :] = weights
            g_ref[here, :] = grad_probs
        scale = 1.0 / jnp.sum(total, axis=0, keepdims=True)
        delta = jnp.sum(delta, axis=0, keepdims=True) * scale
        for part in range(count):
            here = slice(part * chunk, (part + 1) * chunk)
            probs = s_ref[here, :] * scale
            p_ref[here, lanes] = probs.astype(jnp.bfloat16)
            d_ref[here, lanes] = (probs * (g_ref[here, :] - delta)).astype(jnp.bfloat16)

    rows_here = pl.ds(start, window)
    acc_ref[0, rows_here, :] += inverse * jnp.dot(
        d_ref[...], stack(q_ref, 0, heads), preferred_element_type=jnp.float32
    )
    acc_ref[1, rows_here, :] += jnp.dot(
        p_ref[...], stack(o_ref, 0, heads), preferred_element_type=jnp.float32
    )
    grad_t = lax.dot_general(
        k_ref[rows_here, :],
        d_ref[...],
        (((0,), (0,)), ((), ())),
        preferred_element_type=jnp.float32,
    )
    for head in range(heads):
        block = grad_t[:, head * rows : (head + 1) * rows]
        dq_ref[:, head * HEAD_FEATURES : (head + 1) * HEAD_FEATURES] = (
            block.T * inverse
        ).astype(jnp.bfloat16)

    @pl.when(side == 1)
    def _():
        dkv_ref[...] = acc_ref[...].astype(jnp.bfloat16)


def attend(info, queries, grads, keys, values):
    tokens, width = queries.shape
    rows = tokens // 2
    span, kv = keys.shape
    groups = kv // HEAD_FEATURES
    wide = width // groups
    window = span - rows
    stacked = rows * wide // HEAD_FEATURES
    query_spec = pl.BlockSpec((rows, wide), lambda group, side, info_ref: (side, group))
    key_spec = pl.BlockSpec((span, HEAD_FEATURES), lambda group, side, info_ref: (0, group))
    return pl.pallas_call(
        attention_kernel,
        grid_spec=pltpu.PrefetchScalarGridSpec(
            num_scalar_prefetch=1,
            grid=(groups, 2),
            in_specs=[query_spec, query_spec, key_spec, key_spec],
            out_specs=(
                query_spec,
                pl.BlockSpec(
                    (2, span, HEAD_FEATURES), lambda group, side, info_ref: (0, 0, group)
                ),
            ),
            scratch_shapes=[
                pltpu.VMEM((window, rows), jnp.float32),
                pltpu.VMEM((window, 2 * rows), jnp.float32),
                pltpu.VMEM((window, 2 * rows), jnp.float32),
                pltpu.VMEM((window, stacked), jnp.bfloat16),
                pltpu.VMEM((window, stacked), jnp.bfloat16),
                pltpu.VMEM((2, span, HEAD_FEATURES), jnp.float32),
            ],
        ),
        out_shape=(
            jax.ShapeDtypeStruct((tokens, width), jnp.bfloat16),
            jax.ShapeDtypeStruct((2, span, kv), jnp.bfloat16),
        ),
        name="attention_backward",
    )(info, queries, grads, keys, values)


def return_kernel(
    chips, reach, dq_ref, dkv_ref, full_ref, parts_ref, send_sems, recv_sems, pair_send, pair_recv, local_sem
):
    me = lax.axis_index("seq")
    chip = me // 2
    core = lax.rem(me, 2)
    partner = me + 1 - 2 * core
    barrier = pltpu.get_barrier_semaphore()
    greet_halo(barrier, chips, reach, 1)
    pl.semaphore_wait(barrier, 2 * reach + 1)

    rows = full_ref.shape[0]
    wide = dq_ref.shape[1]
    half = dkv_ref.shape[2]
    kv_lanes = pl.ds(pl.multiple_of(core * half, half), half)
    waits = []
    for behind in range(reach, -1, -1):
        for cross in range(2):
            to_core = core if cross == 0 else 1 - core
            slot = pl.multiple_of(((reach - behind) * 2 + to_core) * rows, rows)
            source = dkv_ref.at[:, pl.ds(slot, rows), :]
            target = parts_ref.at[behind, :, :, kv_lanes]
            index = behind * 2 + cross
            if index == 0:
                copy = pltpu.make_async_copy(source, target, local_sem.at[0])
            else:
                copy = pltpu.make_async_remote_copy(
                    src_ref=source,
                    dst_ref=target,
                    send_sem=send_sems.at[index],
                    recv_sem=recv_sems.at[index],
                    device_id={"seq": lax.rem(chip + chips - behind, chips) * 2 + to_core},
                    device_id_type=MESH,
                )
            copy.start()
            waits.append(copy)
    lanes = pl.ds(pl.multiple_of(core * wide, wide), wide)
    copy = pltpu.make_async_remote_copy(
        src_ref=dq_ref.at[pl.ds(pl.multiple_of((1 - core) * rows, rows), rows), :],
        dst_ref=full_ref.at[:, lanes],
        send_sem=pair_send,
        recv_sem=pair_recv,
        device_id={"seq": partner},
        device_id_type=MESH,
    )
    copy.start()
    waits.append(copy)
    copy = pltpu.make_async_copy(
        dq_ref.at[pl.ds(pl.multiple_of(core * rows, rows), rows), :],
        full_ref.at[:, lanes],
        local_sem.at[1],
    )
    copy.start()
    waits.append(copy)
    for copy in waits:
        copy.wait()


def give_back(grad_queries, grad_pairs, chips, reach):
    tokens, width = grad_queries.shape
    kv = grad_pairs.shape[2]
    rows = tokens // 2
    links = 2 * (reach + 1)
    sems = pltpu.SemaphoreType.DMA
    anywhere = pl.BlockSpec(memory_space=pl.ANY)
    vmem = pl.BlockSpec(memory_space=pltpu.VMEM)
    return pl.pallas_call(
        functools.partial(return_kernel, chips, reach),
        out_shape=(
            jax.ShapeDtypeStruct((rows, 2 * width), jnp.bfloat16),
            jax.ShapeDtypeStruct((reach + 1, 2, rows, 2 * kv), jnp.bfloat16),
        ),
        in_specs=[vmem, vmem],
        out_specs=(anywhere, anywhere),
        scratch_shapes=[sems((links,)), sems((links,)), sems, sems, sems((2,))],
        compiler_params=pltpu.CompilerParams(collective_id=3, has_side_effects=True),
        name="return_gradients",
    )(grad_queries, grad_pairs)


def contract_trailing(left_rows, right_rows):
    return lax.dot_general(
        left_rows, right_rows, (((1,), (1,)), ((), ())), preferred_element_type=jnp.float32
    )


def body(
    normed_block_input,
    stored_rotated_queries,
    stored_rotated_keys,
    attention_output_gradient,
    frozen_value_weight,
    adapter_down_weight,
    adapter_up_weight,
    packed_document_lengths,
):
    token_rows = normed_block_input.shape[1]
    model_features = normed_block_input.shape[2]
    hidden_activations = normed_block_input.reshape(token_rows, model_features)
    seq_count = lax.axis_size("seq")
    fsdp_count = lax.axis_size("fsdp")
    chips = seq_count // 2
    reach = DOC_MOST // (2 * token_rows)
    up_widened = adapter_up_weight.astype(jnp.float32)

    queries, grads, keys, weight = gather_all(
        stored_rotated_queries[0],
        attention_output_gradient[0],
        stored_rotated_keys[0],
        frozen_value_weight,
        fsdp_count,
    )
    adapter_projection = contract_trailing(hidden_activations, adapter_down_weight)
    adapter_maps = ADAPTER_SCALE * jnp.dot(
        adapter_projection, up_widened, precision=lax.Precision.HIGHEST
    )
    base_value = jnp.dot(hidden_activations, weight, preferred_element_type=jnp.float32)
    adapter_values = (base_value + adapter_maps).astype(jnp.bfloat16)
    values = gather_values(adapter_values)
    info = jnp.concatenate(
        [(lax.axis_index("seq") // 2).astype(jnp.int32)[None], packed_document_lengths[0]]
    )
    grad_queries, grad_pairs = attend(info, queries, grads, keys, values)
    rotated_query_gradient, parts = give_back(grad_queries, grad_pairs, chips, reach)
    summed = parts.astype(jnp.float32).sum(axis=0)
    rotated_key_gradient = summed[0].astype(jnp.bfloat16)
    value_gradient_matrix = summed[1]
    value_grad_low = value_gradient_matrix.astype(jnp.bfloat16)
    adapter_rank_gradient = ADAPTER_SCALE * lax.dot_general(
        value_gradient_matrix, up_widened, (((1,), (1,)), ((), ())), precision=lax.Precision.HIGHEST
    )
    reduced_rank_gradient = adapter_rank_gradient.astype(jnp.bfloat16)
    overall_token_count = token_rows * seq_count * fsdp_count
    down_shard = (
        lax.dot_general(
            reduced_rank_gradient,
            hidden_activations,
            (((0,), (0,)), ((), ())),
            preferred_element_type=jnp.float32,
        )
        / overall_token_count
    )
    up_shard = (
        ADAPTER_SCALE
        * jnp.dot(adapter_projection.T, value_gradient_matrix, precision=lax.Precision.HIGHEST)
        / overall_token_count
    )
    adapter_down_gradient, adapter_up_gradient, input_gradient = sum_over_mesh(
        down_shard,
        up_shard,
        value_grad_low,
        reduced_rank_gradient,
        adapter_down_weight,
        weight,
        seq_count,
        fsdp_count,
    )
    return (
        input_gradient[None],
        rotated_query_gradient[None],
        rotated_key_gradient[None],
        adapter_down_gradient,
        adapter_up_gradient,
    )


def solution(mesh):
    placed = (
        P("fsdp", "seq", None),
        P("fsdp", "seq", None),
        P("fsdp", "seq", None),
        P("fsdp", "seq", None),
        P("fsdp", None),
        P(),
        P(),
        P("fsdp", None),
    )
    return jax.shard_map(
        body,
        mesh=mesh,
        in_specs=placed,
        out_specs=(
            P("fsdp", "seq", None),
            P("fsdp", "seq", None),
            P("fsdp", "seq", None),
            P(),
            P(),
        ),
        check_vma=False,
    )
```

```python
import functools

import jax
import jax.numpy as jnp
from jax import lax
from jax.experimental import pallas as pl
from jax.experimental.pallas import tpu as pltpu
from jax.sharding import PartitionSpec as P

HEAD_FEATURES = 128


ADAPTER_SCALE = 2.0
NEG_FILL = -1e30
LOG2_E = 1.4426950408889634
DOCS = 8
DOC_MOST = 1024


MESH = pl.DeviceIdType.MESH
SUM_LANES = 256
SUM_WIDE = 384


def sum_kernel(
    chips,
    depth,
    down_ref,
    up_ref,
    grad_ref,
    rank_ref,
    map_ref,
    weight_ref,
    down_out,
    up_out,
    input_out,
    parts_ref,
    pair_in,
    pair_total,
    chip_in,
    depth_in,
    final_ref,
    weight_in,
    weight_sems,
    pair_send,
    pair_recv,
    chip_send,
    chip_recv,
    depth_send,
    depth_recv,
    give_send,
    give_recv,
    hand_send,
    hand_recv,
):
    me = lax.axis_index("seq")
    layer = lax.axis_index("fsdp")
    chip = me // 2
    core = lax.rem(me, 2)
    partner = chip * 2 + 1 - core
    tiles = weight_sems.shape[0]
    tile = weight_ref.shape[0] // tiles

    def chip_peer(offset):
        return lax.rem(chip + offset, chips) * 2 + core

    def depth_peer(offset):
        return lax.rem(layer + offset, depth)

    def weight_copy(index):
        rows = pl.ds(pl.multiple_of(index * tile, tile), tile)
        return pltpu.make_async_copy(
            weight_ref.at[rows, :], weight_in.at[rows, :], weight_sems.at[index]
        )

    for index in range(tiles):
        weight_copy(index).start()

    barrier = pltpu.get_barrier_semaphore()
    pl.semaphore_signal(barrier, inc=1, device_id={"seq": partner}, device_id_type=MESH)
    for offset in range(1, chips):
        pl.semaphore_signal(
            barrier, inc=1, device_id={"seq": chip_peer(offset)}, device_id_type=MESH
        )
    for offset in range(1, depth):
        pl.semaphore_signal(
            barrier, inc=1, device_id={"fsdp": depth_peer(offset)}, device_id_type=MESH
        )

    spare = up_ref.shape[1] // 128
    parts_ref[:, :, :, SUM_LANES:] = jnp.zeros_like(parts_ref[:, :, :, SUM_LANES:])
    for index in range(spare):
        parts_ref[index // 2, index % 2, :, SUM_LANES:] = up_ref[
            :, index * 128 : (index + 1) * 128
        ]
    for index in range(2 * chips):
        parts_ref[index // 2, index % 2, :, :SUM_LANES] = down_ref[
            :, index * SUM_LANES : (index + 1) * SUM_LANES
        ]
    pl.semaphore_wait(barrier, chips + depth - 1)

    pair = pltpu.make_async_remote_copy(
        src_ref=parts_ref.at[:, 1 - core],
        dst_ref=pair_in,
        send_sem=pair_send,
        recv_sem=pair_recv,
        device_id={"seq": partner},
        device_id_type=MESH,
    )
    pair.start()
    pair.wait()

    def add_pair(index, carry):
        pair_total[index] = (parts_ref[index, core] + pair_in[index]).astype(jnp.bfloat16)
        return carry

    lax.fori_loop(0, chips, add_pair, 0)

    copies = []
    for offset in range(1, chips):
        target = lax.rem(chip + offset, chips)
        copy = pltpu.make_async_remote_copy(
            src_ref=pair_total.at[target],
            dst_ref=chip_in.at[offset - 1],
            send_sem=chip_send.at[offset - 1],
            recv_sem=chip_recv.at[offset - 1],
            device_id={"seq": chip_peer(offset)},
            device_id_type=MESH,
        )
        copy.start()
        copies.append(copy)

    def project(index, carry):
        weight_copy(index).wait()
        lanes = pl.ds(pl.multiple_of(index * tile, tile), tile)
        gradient = lax.dot_general(
            grad_ref[...],
            weight_in[lanes, :],
            (((1,), (1,)), ((), ())),
            preferred_element_type=jnp.float32,
        ) + jnp.dot(rank_ref[...], map_ref[:, lanes], preferred_element_type=jnp.float32)
        input_out[:, lanes] = gradient.astype(jnp.bfloat16)
        return carry

    lax.fori_loop(0, tiles, project, 0)

    for copy in copies:
        copy.wait()
    total = pair_total[chip].astype(jnp.float32)
    for offset in range(chips - 1):
        total = total + chip_in[offset].astype(jnp.float32)
    depth_in[layer] = total.astype(jnp.bfloat16)

    copies = []
    for offset in range(1, depth):
        copies.append(
            pltpu.make_async_remote_copy(
                src_ref=depth_in.at[layer],
                dst_ref=depth_in.at[layer],
                send_sem=depth_send.at[offset - 1],
                recv_sem=depth_recv.at[offset - 1],
                device_id={"fsdp": depth_peer(offset)},
                device_id_type=MESH,
            )
        )
    for copy in copies:
        copy.start()
    for offset, copy in enumerate(copies, 1):
        source = lax.rem(layer + depth - offset, depth)
        copy.wait_send()
        pltpu.make_async_remote_copy(
            src_ref=depth_in.at[source],
            dst_ref=depth_in.at[source],
            send_sem=depth_send.at[offset - 1],
            recv_sem=depth_recv.at[offset - 1],
            device_id={"fsdp": depth_peer(offset)},
            device_id_type=MESH,
        ).wait_recv()
    final = depth_in[0].astype(jnp.float32)
    for index in range(1, depth):
        final = final + depth_in[index].astype(jnp.float32)
    final_ref[chip, core] = final.astype(jnp.bfloat16)

    gives = []
    for offset in range(1, chips):
        copy = pltpu.make_async_remote_copy(
            src_ref=final_ref.at[chip, core],
            dst_ref=final_ref.at[chip, core],
            send_sem=give_send.at[offset - 1],
            recv_sem=give_recv.at[offset - 1],
            device_id={"seq": chip_peer(offset)},
            device_id_type=MESH,
        )
        copy.start()
        gives.append(copy)

    def hand_copy(offset, sender):
        owner = lax.rem(chip + chips - offset, chips)
        return pltpu.make_async_remote_copy(
            src_ref=final_ref.at[owner, sender],
            dst_ref=final_ref.at[owner, sender],
            send_sem=hand_send.at[offset],
            recv_sem=hand_recv.at[offset],
            device_id={"seq": partner},
            device_id_type=MESH,
        )

    hands = []
    for offset in range(chips):
        if offset:
            owner = lax.rem(chip + chips - offset, chips)
            pltpu.make_async_remote_copy(
                src_ref=final_ref.at[owner, core],
                dst_ref=final_ref.at[owner, core],
                send_sem=give_send.at[offset - 1],
                recv_sem=give_recv.at[offset - 1],
                device_id={"seq": chip_peer(offset)},
                device_id_type=MESH,
            ).wait_recv()
        hand = hand_copy(offset, core)
        hand.start()
        hands.append(hand)
    for copy in gives:
        copy.wait_send()
    for offset, hand in enumerate(hands):
        hand.wait_send()
        hand_copy(offset, 1 - core).wait_recv()
    for index in range(2 * chips):
        down_out[:, index * SUM_LANES : (index + 1) * SUM_LANES] = final_ref[
            index // 2, index % 2, :, :SUM_LANES
        ].astype(jnp.float32)
    for index in range(spare):
        up_out[:, index * 128 : (index + 1) * 128] = final_ref[
            index // 2, index % 2, :, SUM_LANES:
        ].astype(jnp.float32)


def sum_over_mesh(
    down_shard, up_shard, value_grad, rank_grad, down_weight, weight, seq_count, fsdp_count
):
    chips = seq_count // 2
    rank = down_shard.shape[0]
    block = (rank, SUM_WIDE)
    tiles = 8
    sems = pltpu.SemaphoreType.DMA
    vmem = pl.BlockSpec(memory_space=pltpu.VMEM)
    return pl.pallas_call(
        functools.partial(sum_kernel, chips, fsdp_count),
        out_shape=(
            jax.ShapeDtypeStruct(down_shard.shape, jnp.float32),
            jax.ShapeDtypeStruct(up_shard.shape, jnp.float32),
            jax.ShapeDtypeStruct((value_grad.shape[0], weight.shape[0]), jnp.bfloat16),
        ),
        in_specs=[vmem] * 5 + [pl.BlockSpec(memory_space=pl.ANY)],
        out_specs=(vmem,) * 3,
        scratch_shapes=[
            pltpu.VMEM((chips, 2) + block, jnp.float32),
            pltpu.VMEM((chips,) + block, jnp.float32),
            pltpu.VMEM((chips,) + block, jnp.bfloat16),
            pltpu.VMEM((chips - 1,) + block, jnp.bfloat16),
            pltpu.VMEM((fsdp_count,) + block, jnp.bfloat16),
            pltpu.VMEM((chips, 2) + block, jnp.bfloat16),
            pltpu.VMEM(weight.shape, jnp.bfloat16),
            sems((tiles,)),
            sems,
            sems,
            sems((chips - 1,)),
            sems((chips - 1,)),
            sems((fsdp_count - 1,)),
            sems((fsdp_count - 1,)),
            sems((chips - 1,)),
            sems((chips - 1,)),
            sems((chips,)),
            sems((chips,)),
        ],
        compiler_params=pltpu.CompilerParams(collective_id=0, has_side_effects=True),
        name="adapter_sum",
    )(down_shard, up_shard, value_grad, rank_grad, down_weight, weight)


SIDE = 4


class Place:
    def __init__(self):
        me = lax.axis_index("seq")
        self.chip = me // 2
        self.core = lax.rem(me, 2)
        self.column = lax.rem(self.chip, SIDE)
        self.row = self.chip // SIDE
        self.partner = me + 1 - 2 * self.core

    def along_x(self, offset):
        column = lax.rem(self.column + offset + SIDE, SIDE)
        return (self.row * SIDE + column) * 2 + self.core

    def along_y(self, offset):
        row = lax.rem(self.row + offset + SIDE, SIDE)
        return (row * SIDE + self.column) * 2 + self.core

    def greet(self, barrier):
        peers = [self.partner] + [self.along_x(i) for i in range(1, SIDE)]
        peers += [self.along_y(1), self.along_y(-1)]
        for peer in peers:
            pl.semaphore_signal(barrier, inc=1, device_id={"seq": peer}, device_id_type=MESH)
        return len(peers)


class Halo:
    LINKS = SIDE + 2

    def __init__(self, place, source_ref, target_ref, send_sems, recv_sems, local_sem):
        self.place = place
        self.target_ref = target_ref
        self.send_sems, self.recv_sems = send_sems, recv_sems
        rows, width = source_ref.shape
        half = width // 2
        self.block = 2 * rows
        core = place.core
        first = SIDE * self.block + core * rows
        here = target_ref.at[pl.ds(pl.multiple_of(first, rows), rows), :]
        mine = pl.ds(pl.multiple_of(core * half, half), half)
        theirs = pl.ds(pl.multiple_of((1 - core) * half, half), half)
        self.own = pltpu.make_async_copy(source_ref.at[:, mine], here, local_sem)
        self.pair = pltpu.make_async_remote_copy(
            src_ref=source_ref.at[:, theirs],
            dst_ref=here,
            send_sem=send_sems.at[0],
            recv_sem=recv_sems.at[0],
            device_id={"seq": place.partner},
            device_id_type=MESH,
        )

    def copy(self, index, source, target, peer):
        first = source * self.block
        return pltpu.make_async_remote_copy(
            src_ref=self.target_ref.at[
                pl.ds(pl.multiple_of(first, self.block), self.block), :
            ],
            dst_ref=self.target_ref.at[pl.ds(target * self.block, self.block), :],
            send_sem=self.send_sems.at[index],
            recv_sem=self.recv_sems.at[index],
            device_id={"seq": peer},
            device_id_type=MESH,
        )

    def start(self):
        self.own.start()
        self.pair.start()

    def along_x(self, offset):
        wraps = (self.place.column + offset) // SIDE
        index = 2 if offset == 1 else 3
        copy = self.copy(
            index, SIDE * (1 - wraps), SIDE - offset, self.place.along_x(offset)
        )
        return wraps, copy

    def spread(self):
        place = self.place
        self.own.wait()
        self.pair.wait()
        self.vertical = self.copy(1, SIDE, 0, place.along_y(1))
        self.vertical.start()
        self.sideways = [self.along_x(1), self.along_x(SIDE - 1)]
        for wraps, copy in self.sideways:

            @pl.when(wraps == 0)
            def _():
                copy.start()

        self.vertical.wait_recv()
        for wraps, copy in self.sideways:

            @pl.when(wraps == 1)
            def _():
                copy.start()

    def relay(self):
        place = self.place
        inner = (place.column == 1) | (place.column == 2)
        self.sideways[0][1].wait_recv()
        forward = self.copy(4, SIDE - 1, SIDE - 2, place.along_x(1))

        @pl.when(inner)
        def _():
            forward.start()

        self.sideways[1][1].wait_recv()
        backward = self.copy(5, 1, SIDE - 2, place.along_x(-1))

        @pl.when(inner)
        def _():
            backward.start()

        self.relays = (inner, forward, backward)

    def finish(self):
        inner, forward, backward = self.relays
        left = self.place.column < SIDE // 2

        @pl.when(left)
        def _():
            backward.wait_recv()

        @pl.when(jnp.logical_not(left))
        def _():
            forward.wait_recv()

        @pl.when(inner)
        def _():
            forward.wait_send()
            backward.wait_send()

        self.vertical.wait_send()
        for _, copy in self.sideways:
            copy.wait_send()


def gather_kernel(
    depth,
    q_ref,
    o_ref,
    k_ref,
    w_ref,
    x_ref,
    map_ref,
    up_ref,
    qc_ref,
    oc_ref,
    kc_ref,
    wc_ref,
    low_ref,
    v_ref,
    weight,
    total,
    halo_send,
    halo_recv,
    pair_send,
    pair_recv,
    local_sem,
    store_sem,
    deep_send,
    deep_recv,
    plane_send,
    plane_recv,
    pass_send,
    pass_recv,
):
    place = Place()
    core, partner = place.core, place.partner
    layer = lax.axis_index("fsdp")
    up = lax.rem(layer + 1, depth)
    down = lax.rem(layer + depth - 1, depth)

    barrier = pltpu.get_barrier_semaphore()
    count = place.greet(barrier)
    for peer in (up, down):
        pl.semaphore_signal(barrier, inc=1, device_id={"fsdp": peer}, device_id_type=MESH)
    pl.semaphore_wait(barrier, count + 2)

    shard = w_ref.shape[0]
    group = shard // 4
    part = group // SIDE
    steps = depth // 2
    numbers = 2 * steps - 1
    position = (place.column, place.row)

    def block_at(step, way):
        return lax.rem(layer + depth + (step if way else -step), depth)

    def remote(rows, source_rows, send, recv, peer, source_ref=None):
        return pltpu.make_async_remote_copy(
            src_ref=(weight if source_ref is None else source_ref).at[source_rows, :],
            dst_ref=weight.at[rows, :],
            send_sem=send,
            recv_sem=recv,
            device_id=peer,
            device_id_type=MESH,
        )

    def slice_rows(block, axis, owner, spot):
        first = block * shard + axis * 2 * group + owner * group + spot * part
        return pl.ds(pl.multiple_of(first, part), part)

    def group_rows(block, axis, owner):
        first = block * shard + axis * 2 * group + owner * group
        return pl.ds(pl.multiple_of(first, group), group)

    def deep_copy(step, way, axis):
        rows = slice_rows(block_at(step - 1, way), axis, core, position[axis])
        peer = {"fsdp": down if way else up}
        sems = deep_send.at[way, step - 1, axis], deep_recv.at[way, step - 1, axis]
        if step == 1:
            source = slice_rows(0, axis, core, position[axis])
            return remote(rows, source, *sems, peer, w_ref)
        return remote(rows, rows, *sems, peer)

    def deep_got(step, way, axis):
        rows = slice_rows(block_at(step, way), axis, core, position[axis])
        sems = deep_send.at[way, step - 1, axis], deep_recv.at[way, step - 1, axis]
        return remote(rows, rows, *sems, {"fsdp": up})

    def toward(axis, offset):
        return {"seq": place.along_y(offset) if axis else place.along_x(offset)}

    def plane_copy(number, block, axis, kind, sending):
        step_forward = 1 if kind == 0 or (kind == 2 and number % 2) else -1
        if kind == 2:
            spot = -step_forward if sending else 2
        else:
            spot = 0 if sending else -step_forward
        spot = lax.rem(position[axis] + spot + SIDE, SIDE)
        rows = slice_rows(block, axis, core, spot)
        sems = plane_send.at[axis, number - 1, kind], plane_recv.at[axis, number - 1, kind]
        return remote(rows, rows, *sems, toward(axis, step_forward))

    def pass_copy(number, block, axis, owner):
        rows = group_rows(block, axis, owner)
        sems = pass_send.at[axis, number - 1], pass_recv.at[axis, number - 1]
        return remote(rows, rows, *sems, {"seq": partner})

    sent = []

    def go(copy):
        copy.start()
        sent.append(copy)

    for axis in range(2):
        for way in range(2):
            go(deep_copy(1, way, axis))
    halo = Halo(place, k_ref, kc_ref, halo_send, halo_recv, local_sem.at[2])
    halo.start()
    rows = q_ref.shape[0]
    wide = q_ref.shape[1] // 2
    here = pl.ds(pl.multiple_of(core * rows, rows), rows)
    mine = pl.ds(pl.multiple_of(core * wide, wide), wide)
    theirs = pl.ds(pl.multiple_of((1 - core) * wide, wide), wide)
    pairs = []
    locals_ = []
    for index, (source_ref, target_ref) in enumerate(((q_ref, qc_ref), (o_ref, oc_ref))):
        copy = pltpu.make_async_remote_copy(
            src_ref=source_ref.at[:, theirs],
            dst_ref=target_ref.at[here, :],
            send_sem=pair_send.at[index],
            recv_sem=pair_recv.at[index],
            device_id={"seq": partner},
            device_id_type=MESH,
        )
        copy.start()
        pairs.append(copy)
        copy = pltpu.make_async_copy(
            source_ref.at[:, mine], target_ref.at[here, :], local_sem.at[index]
        )
        copy.start()
        locals_.append(copy)

    def store(index, source, block):
        target = wc_ref.at[pl.ds(pl.multiple_of(block * shard, shard), shard), :]
        copy = pltpu.make_async_copy(source, target, store_sem.at[index])
        copy.start()
        locals_.append(copy)

    def project(block, rows_of_weight):
        lanes = pl.ds(pl.multiple_of(block * shard, shard), shard)
        return jnp.dot(x_ref[:, lanes], rows_of_weight, preferred_element_type=jnp.float32)

    store(0, w_ref, layer)
    halo.spread()
    low = lax.dot_general(
        x_ref[...],
        map_ref[...],
        (((1,), (1,)), ((), ())),
        preferred_element_type=jnp.float32,
    )
    low_ref[...] = low
    total[...] = project(layer, w_ref[...]) + ADAPTER_SCALE * jnp.dot(
        low,
        up_ref[...].astype(jnp.float32),
        precision=lax.Precision.HIGHEST,
        preferred_element_type=jnp.float32,
    )

    blocks = {}
    members = {}
    for number in range(1, numbers + 1):
        step, way = (number + 1) // 2, (number - 1) % 2
        blocks[number] = block_at(step, way)
        members.setdefault(step, []).append(number)

    def pass_on(step):
        for number in members.get(step, ()):
            for axis in range(2):
                kind = 0 if number % 2 else 1
                plane_copy(number, blocks[number], axis, kind, False).wait_recv()
                go(plane_copy(number, blocks[number], axis, 2, True))

    def hand_over(step):
        for number in members.get(step, ()):
            for axis in range(2):
                kind = 1 if number % 2 else 0
                plane_copy(number, blocks[number], axis, kind, False).wait_recv()
                plane_copy(number, blocks[number], axis, 2, False).wait_recv()
                go(pass_copy(number, blocks[number], axis, core))

    def use(step):
        for number in members.get(step, ()):
            block = blocks[number]
            for axis in range(2):
                pass_copy(number, block, axis, 1 - core).wait_recv()
            first = pl.ds(pl.multiple_of(block * shard, shard), shard)
            store(number, weight.at[first, :], block)
            total[...] += project(block, weight[first, :])

    for step in range(1, steps + 1):
        for number in members[step]:
            way = (number - 1) % 2
            for axis in range(2):
                came = axis if step == steps else way
                deep_got(step, came, axis).wait_recv()
                if step + 1 < steps or (step + 1 == steps and axis == way):
                    go(deep_copy(step + 1, way, axis))
                for kind in range(2):
                    go(plane_copy(number, blocks[number], axis, kind, True))
        pass_on(step - 1)
        if step == 2:
            halo.relay()
        hand_over(step - 2)
        use(step - 3)
    hand_over(steps - 1)
    pass_on(steps)
    use(steps - 2)
    use(steps - 1)
    hand_over(steps)
    use(steps)
    v_ref[...] = total[...].astype(jnp.bfloat16)

    halo.finish()
    for copy in locals_:
        copy.wait()
    for copy in pairs:
        copy.wait()
    for copy in sent:
        copy.wait_send()


def gather_all(queries, grads, keys, weight, hidden, down_weight, up_weight, depth):
    rows, width = queries.shape
    kv = keys.shape[1]
    sems = pltpu.SemaphoreType.DMA
    steps = depth // 2
    numbers = 2 * steps - 1
    anywhere = pl.BlockSpec(memory_space=pl.ANY)
    vmem = pl.BlockSpec(memory_space=pltpu.VMEM)
    dtype = jnp.bfloat16
    whole = (depth * weight.shape[0], weight.shape[1])
    return pl.pallas_call(
        functools.partial(gather_kernel, depth),
        out_shape=(
            jax.ShapeDtypeStruct((2 * rows, width // 2), dtype),
            jax.ShapeDtypeStruct((2 * rows, width // 2), dtype),
            jax.ShapeDtypeStruct(((SIDE + 1) * 2 * rows, kv // 2), dtype),
            jax.ShapeDtypeStruct(whole, dtype),
            jax.ShapeDtypeStruct((rows, down_weight.shape[0]), jnp.float32),
            jax.ShapeDtypeStruct((rows, kv), dtype),
        ),
        in_specs=[vmem] * 7,
        out_specs=(anywhere,) * 4 + (vmem,) * 2,
        scratch_shapes=[
            pltpu.VMEM(whole, dtype),
            pltpu.VMEM((rows, kv), jnp.float32),
            sems((Halo.LINKS,)),
            sems((Halo.LINKS,)),
            sems((2,)),
            sems((2,)),
            sems((3,)),
            sems((numbers + 1,)),
            sems((2, steps, 2)),
            sems((2, steps, 2)),
            sems((2, numbers, 3)),
            sems((2, numbers, 3)),
            sems((2, numbers)),
            sems((2, numbers)),
        ],
        compiler_params=pltpu.CompilerParams(collective_id=1, has_side_effects=True),
        name="gather_inputs",
    )(queries, grads, keys, weight, hidden, down_weight, up_weight)


class Window:
    def __init__(self, chips):
        self.chips = chips
        me = lax.axis_index("seq")
        self.chip = me // 2
        self.core = lax.rem(me, 2)
        self.partner = me + 1 - 2 * self.core

    def peer(self, away, cross):
        chip = lax.rem(self.chip + self.chips + away, self.chips)
        return chip * 2 + (1 - self.core if cross else self.core)

    def links(self):
        return [(away, cross) for away in range(SIDE, -1, -1) for cross in range(2)][:-2] + [(0, 1)]

    def greet(self, barrier):
        peers = [self.peer(away, cross) for away, cross in self.links()]
        peers += [self.peer(-away, cross) for away, cross in self.links() if away]
        for peer in peers:
            pl.semaphore_signal(barrier, inc=1, device_id={"seq": peer}, device_id_type=MESH)
        pl.semaphore_wait(barrier, len(peers))


def attention_kernel(
    chips,
    info_ref,
    q_ref,
    o_ref,
    k_ref,
    v_ref,
    dq_ref,
    dk_ref,
    dv_ref,
    bias_ref,
    s_ref,
    g_ref,
    p_ref,
    d_ref,
    acc_ref,
    values_ref,
    give_ref,
    back_ref,
    query_ref,
    came_ref,
    value_send,
    value_recv,
    back_send,
    back_recv,
    query_send,
    query_recv,
):
    net = Window(chips)
    core = net.core
    chip = info_ref[0]
    group = pl.program_id(0)
    side = pl.program_id(1)
    groups = 2
    rows = q_ref.shape[0]
    wide = q_ref.shape[1]
    heads = wide // HEAD_FEATURES
    window = bias_ref.shape[0]
    span = k_ref.shape[0]
    start = pl.multiple_of(side * rows, rows)
    inverse = HEAD_FEATURES ** (-0.5)
    steep = inverse * LOG2_E
    chunk = 128
    count = window // chunk

    def kv_lanes(owner, head):
        first = (owner * groups + head) * HEAD_FEATURES
        return pl.ds(pl.multiple_of(first, HEAD_FEATURES), HEAD_FEATURES)

    def slot(away, owner):
        return pl.ds(pl.multiple_of(((SIDE - away) * 2 + owner) * rows, rows), rows)

    def value_copy(head, away, cross):
        to_core = 1 - core if cross else core
        index = away * 2 + cross
        return pltpu.make_async_remote_copy(
            src_ref=v_ref.at[:, kv_lanes(to_core, head)],
            dst_ref=values_ref.at[head, slot(away, core), :],
            send_sem=value_send.at[head, index],
            recv_sem=value_recv.at[head, index],
            device_id={"seq": net.peer(away, cross)},
            device_id_type=MESH,
        )

    def back_copy(head, away, cross):
        to_core = 1 - core if cross else core
        index = away * 2 + cross
        return pltpu.make_async_remote_copy(
            src_ref=give_ref.at[head, :, slot(away, to_core), :],
            dst_ref=back_ref.at[away, :, :, kv_lanes(core, head)],
            send_sem=back_send.at[head, index],
            recv_sem=back_recv.at[head, index],
            device_id={"seq": net.peer(-away, cross)},
            device_id_type=MESH,
        )

    def query_copy(head):
        return pltpu.make_async_remote_copy(
            src_ref=query_ref.at[head, 1 - core],
            dst_ref=came_ref.at[head],
            send_sem=query_send.at[head],
            recv_sem=query_recv.at[head],
            device_id={"seq": net.partner},
            device_id_type=MESH,
        )

    @pl.when((group == 0) & (side == 0))
    def _():
        net.greet(pltpu.get_barrier_semaphore())
        for head in range(groups):
            for link in net.links():
                value_copy(head, *link).start()
        for head in range(groups):
            values_ref[head, slot(0, core), :] = v_ref[:, kv_lanes(core, head)]

    @pl.when(side == 0)
    def _():
        acc_ref[...] = jnp.zeros_like(acc_ref)

    for head in range(groups):

        @pl.when((group == head) & (side == 0))
        def _():
            for link in net.links():
                value_copy(head, *link).wait_recv()

    q_place = chip * (2 * rows) + start + lax.broadcasted_iota(jnp.int32, (1, rows), 1)
    finish = jnp.int32(0)
    opening = jnp.zeros((1, rows), jnp.int32)
    for index in range(DOCS):
        finish = finish + info_ref[1 + index]
        opening = jnp.where(q_place >= finish, finish, opening)
    for part in range(count):
        k_place = (
            chip * (2 * rows)
            - (span - 2 * rows)
            + start
            + part * chunk
            + lax.broadcasted_iota(jnp.int32, (chunk, rows), 0)
        )
        allowed = (k_place >= opening) & (k_place <= q_place)
        bias_ref[part * chunk : (part + 1) * chunk, :] = jnp.where(allowed, 0.0, NEG_FILL)

    def stack(ref, first, number):
        return jnp.concatenate(
            [
                ref[:, (first + i) * HEAD_FEATURES : (first + i + 1) * HEAD_FEATURES]
                for i in range(number)
            ],
            axis=0,
        )

    def fold(values):
        return values.reshape(chunk // 8, 8, values.shape[1])

    trailing = (((1,), (1,)), ((), ()))
    for pair in range(heads // 2):
        q_pair = stack(q_ref, 2 * pair, 2)
        o_pair = stack(o_ref, 2 * pair, 2)
        lanes = slice(pair * 2 * rows, (pair + 1) * 2 * rows)
        peak = None
        for part in range(count):
            here = slice(part * chunk, (part + 1) * chunk)
            scores = lax.dot_general(
                k_ref[pl.ds(start + part * chunk, chunk), :],
                q_pair,
                trailing,
                preferred_element_type=jnp.float32,
            )
            bias = bias_ref[here, :]
            scores = scores + jnp.concatenate([bias, bias], axis=1)
            s_ref[here, :] = scores
            high = jnp.max(fold(scores), axis=0)
            peak = high if peak is None else jnp.maximum(peak, high)
        peak = jnp.max(peak, axis=0, keepdims=True)
        total = jnp.zeros((8, 2 * rows), jnp.float32)
        delta = jnp.zeros((8, 2 * rows), jnp.float32)
        for part in range(count):
            here = slice(part * chunk, (part + 1) * chunk)
            weights = jnp.exp2((s_ref[here, :] - peak) * steep)
            grad_probs = lax.dot_general(
                values_ref[group, pl.ds(start + part * chunk, chunk), :],
                o_pair,
                trailing,
                preferred_element_type=jnp.float32,
            )
            total = total + jnp.sum(fold(weights), axis=0)
            delta = delta + jnp.sum(fold(weights * grad_probs), axis=0)
            s_ref[here, :] = weights
            g_ref[here, :] = grad_probs
        scale = 1.0 / jnp.sum(total, axis=0, keepdims=True)
        delta = jnp.sum(delta, axis=0, keepdims=True) * scale
        for part in range(count):
            here = slice(part * chunk, (part + 1) * chunk)
            probs = s_ref[here, :] * scale
            p_ref[here, lanes] = probs.astype(jnp.bfloat16)
            d_ref[here, lanes] = (probs * (g_ref[here, :] - delta)).astype(jnp.bfloat16)

    rows_here = pl.ds(start, window)
    acc_ref[0, rows_here, :] += inverse * jnp.dot(
        d_ref[...], stack(q_ref, 0, heads), preferred_element_type=jnp.float32
    )
    acc_ref[1, rows_here, :] += jnp.dot(
        p_ref[...], stack(o_ref, 0, heads), preferred_element_type=jnp.float32
    )

    for head in range(groups):

        @pl.when((group == head) & (side == 1))
        def _():
            give_ref[head] = acc_ref[...].astype(jnp.bfloat16)
            for link in net.links():
                back_copy(head, *link).start()
            back_ref[0, :, :, kv_lanes(core, head)] = give_ref[head, :, slot(0, core), :]

    grad_t = lax.dot_general(
        k_ref[rows_here, :],
        d_ref[...],
        (((0,), (0,)), ((), ())),
        preferred_element_type=jnp.float32,
    )
    for head in range(heads):
        block = grad_t[:, head * rows : (head + 1) * rows]
        query_ref[group, side, :, head * HEAD_FEATURES : (head + 1) * HEAD_FEATURES] = (
            block.T * inverse
        ).astype(jnp.bfloat16)

    for head in range(groups):

        @pl.when((group == head) & (side == 1))
        def _():
            query_copy(head).start()

    @pl.when((group == groups - 1) & (side == 1))
    def _():
        for head in range(groups):
            here = pl.ds(pl.multiple_of((core * groups + head) * wide, wide), wide)
            there = pl.ds(pl.multiple_of(((1 - core) * groups + head) * wide, wide), wide)
            query_copy(head).wait()
            dq_ref[:, here] = query_ref[head, core]
            dq_ref[:, there] = came_ref[head]
        for head in range(groups):
            for link in net.links():
                back_copy(head, *link).wait()
                value_copy(head, *link).wait_send()
        grad_k = back_ref[0, 0].astype(jnp.float32)
        grad_v = back_ref[0, 1].astype(jnp.float32)
        for away in range(1, SIDE + 1):
            grad_k = grad_k + back_ref[away, 0].astype(jnp.float32)
            grad_v = grad_v + back_ref[away, 1].astype(jnp.float32)
        dk_ref[...] = grad_k.astype(jnp.bfloat16)
        dv_ref[...] = grad_v


def attend(info, queries, grads, keys, values, chips):
    tokens, width = queries.shape
    rows = tokens // 2
    span, kv = keys.shape
    groups = kv // HEAD_FEATURES
    wide = width // groups
    window = span - rows
    stacked = rows * wide // HEAD_FEATURES
    links = 2 * (SIDE + 1)
    sems = pltpu.SemaphoreType.DMA
    query_spec = pl.BlockSpec((rows, wide), lambda group, side, info_ref: (side, group))
    key_spec = pl.BlockSpec((span, HEAD_FEATURES), lambda group, side, info_ref: (0, group))

    def still(shape):
        return pl.BlockSpec(shape, lambda group, side, info_ref: (0, 0))

    return pl.pallas_call(
        functools.partial(attention_kernel, chips),
        grid_spec=pltpu.PrefetchScalarGridSpec(
            num_scalar_prefetch=1,
            grid=(groups, 2),
            in_specs=[query_spec, query_spec, key_spec, still(values.shape)],
            out_specs=(still((rows, 2 * width)), still(values.shape), still(values.shape)),
            scratch_shapes=[
                pltpu.VMEM((window, rows), jnp.float32),
                pltpu.VMEM((window, 2 * rows), jnp.float32),
                pltpu.VMEM((window, 2 * rows), jnp.float32),
                pltpu.VMEM((window, stacked), jnp.bfloat16),
                pltpu.VMEM((window, stacked), jnp.bfloat16),
                pltpu.VMEM((2, span, HEAD_FEATURES), jnp.float32),
                pltpu.VMEM((groups, span, HEAD_FEATURES), jnp.bfloat16),
                pltpu.VMEM((groups, 2, span, HEAD_FEATURES), jnp.bfloat16),
                pltpu.VMEM((SIDE + 1, 2) + values.shape, jnp.bfloat16),
                pltpu.VMEM((groups, 2, rows, wide), jnp.bfloat16),
                pltpu.VMEM((groups, rows, wide), jnp.bfloat16),
                sems((groups, links)),
                sems((groups, links)),
                sems((groups, links)),
                sems((groups, links)),
                sems((groups,)),
                sems((groups,)),
            ],
        ),
        out_shape=(
            jax.ShapeDtypeStruct((rows, 2 * width), jnp.bfloat16),
            jax.ShapeDtypeStruct(values.shape, jnp.bfloat16),
            jax.ShapeDtypeStruct(values.shape, jnp.float32),
        ),
        compiler_params=pltpu.CompilerParams(collective_id=3, has_side_effects=True),
        name="attention_backward",
    )(info, queries, grads, keys, values)


def contract_trailing(left_rows, right_rows):
    return lax.dot_general(
        left_rows, right_rows, (((1,), (1,)), ((), ())), preferred_element_type=jnp.float32
    )


def body(
    normed_block_input,
    stored_rotated_queries,
    stored_rotated_keys,
    attention_output_gradient,
    frozen_value_weight,
    adapter_down_weight,
    adapter_up_weight,
    packed_document_lengths,
):
    token_rows = normed_block_input.shape[1]
    model_features = normed_block_input.shape[2]
    hidden_activations = normed_block_input.reshape(token_rows, model_features)
    seq_count = lax.axis_size("seq")
    fsdp_count = lax.axis_size("fsdp")
    chips = seq_count // 2
    up_widened = adapter_up_weight.astype(jnp.float32)

    queries, grads, keys, weight, adapter_projection, adapter_values = gather_all(
        stored_rotated_queries[0],
        attention_output_gradient[0],
        stored_rotated_keys[0],
        frozen_value_weight,
        hidden_activations,
        adapter_down_weight,
        adapter_up_weight,
        fsdp_count,
    )
    info = jnp.concatenate(
        [(lax.axis_index("seq") // 2).astype(jnp.int32)[None], packed_document_lengths[0]]
    )
    rotated_query_gradient, rotated_key_gradient, value_gradient_matrix = attend(
        info, queries, grads, keys, adapter_values, chips
    )
    value_grad_low = value_gradient_matrix.astype(jnp.bfloat16)
    adapter_rank_gradient = ADAPTER_SCALE * lax.dot_general(
        value_gradient_matrix, up_widened, (((1,), (1,)), ((), ())), precision=lax.Precision.HIGHEST
    )
    reduced_rank_gradient = adapter_rank_gradient.astype(jnp.bfloat16)
    overall_token_count = token_rows * seq_count * fsdp_count
    down_shard = (
        lax.dot_general(
            reduced_rank_gradient,
            hidden_activations,
            (((0,), (0,)), ((), ())),
            preferred_element_type=jnp.float32,
        )
        / overall_token_count
    )
    up_shard = (
        ADAPTER_SCALE
        * jnp.dot(adapter_projection.T, value_gradient_matrix, precision=lax.Precision.HIGHEST)
        / overall_token_count
    )
    adapter_down_gradient, adapter_up_gradient, input_gradient = sum_over_mesh(
        down_shard,
        up_shard,
        value_grad_low,
        reduced_rank_gradient,
        adapter_down_weight,
        weight,
        seq_count,
        fsdp_count,
    )
    return (
        input_gradient[None],
        rotated_query_gradient[None],
        rotated_key_gradient[None],
        adapter_down_gradient,
        adapter_up_gradient,
    )


def solution(mesh):
    placed = (
        P("fsdp", "seq", None),
        P("fsdp", "seq", None),
        P("fsdp", "seq", None),
        P("fsdp", "seq", None),
        P("fsdp", None),
        P(),
        P(),
        P("fsdp", None),
    )
    return jax.shard_map(
        body,
        mesh=mesh,
        in_specs=placed,
        out_specs=(
            P("fsdp", "seq", None),
            P("fsdp", "seq", None),
            P("fsdp", "seq", None),
            P(),
            P(),
        ),
        check_vma=False,
    )
```
